512 devices in a mesh: node: 16 (over x, y), rows: 32 (over z, core).
Axes of the slice: x: 4, y: 4, z: 16, core: 2. Of those that a mesh axis runs over, the one named last changes fastest.
Arguments:
- subspace: bfloat16 [24576, 256], P('rows'), may hold values from -6 to 6
- inverse: bfloat16 [16, 2, 24576, 768], P('node', None, 'rows')
- weights: float32 [16, 2], P('node'), may hold values from 0.25 to 1
- diag_tiles: float32 [24576, 128], P('rows'), may hold values from -0.5 to 0.5
- upper_tiles: float32 [24576, 128], P('rows'), may hold values from -0.5 to 0.5
Outputs:
- subspace_out: float32 [24576, 256], P('rows')
- projected: float32 [2, 256, 256], replicated
The draws below stay inside these ranges and needn't reach their ends.
All inputs are finite; a program needn't handle non-finite values.
Results may differ from the reference program's by a relative error of at most 0.0025.
Values may be sent and summed in bfloat16 or wider, within the bound.
A program may use at most 64 MiB of HBM per device.

```python
import math
import jax
import jax.numpy as jnp
from jax import lax

HALF_BAND = 128
VECTORS = 256
ROWS_DEV = 768
ITERS = 2
NODES = 16
ORDER = 24576


def draw_inverse(key, part):
    noise_key = jax.random.fold_in(key, 7)
    spread = 0.866 / math.sqrt(ROWS_DEV)
    noise = jax.random.uniform(noise_key, (NODES, 2, ORDER, ROWS_DEV), jnp.float32, -spread, spread)
    row_index = lax.broadcasted_iota(jnp.int32, (ORDER, ROWS_DEV), 0) % ROWS_DEV
    column_index = lax.broadcasted_iota(jnp.int32, (ORDER, ROWS_DEV), 1)
    identity = (row_index == column_index).astype(jnp.float32)
    real_mark = (lax.broadcasted_iota(jnp.int32, (2,), 0) == 0).astype(jnp.float32)
    return (noise + identity[None, None] * real_mark[None, :, None, None]).astype(jnp.bfloat16)


def level_of(stream_key, dims, pieces, low, largest):
    gain, own = 1.0, jax.random.fold_in(stream_key, 6)
    for dim, blocks in pieces:
        heights = jnp.exp(jax.random.uniform(jax.random.fold_in(own, dim), (blocks,), jnp.float32, low / len(pieces), largest / len(pieces)))
        gain = gain * jnp.repeat(heights, dims[dim] // blocks).reshape([-1 if axis == dim else 1 for axis in range(len(dims))])
    return gain


def bell_draw(key, extent, deviation, limit, pieces=(), kind=jnp.bfloat16):
    values = jax.random.normal(key, extent, jnp.float32) * deviation
    if len(pieces) > 0:
        values = level_of(key, extent, pieces, -0.22, 0.18) * values
    return jnp.clip(values, min=-limit, max=limit).astype(kind)


def setup_inputs(seed: int = 0) -> dict:
    seeds = jax.random.split(jax.random.key(seed), 6)
    return {
        "subspace": bell_draw(seeds[0], (ORDER, VECTORS), 1.0, 6.0, ((0, 32),)),
        "inverse": draw_inverse(jax.random.fold_in(seeds[5], 71), 0),
        "weights": jnp.clip(0.25 + 0.75 * jax.random.uniform(seeds[2], (NODES, 2), jnp.float32) ** level_of(seeds[2], (NODES, 2), ((0, 16),), -0.2, 0.2), 0.25, 1.0),
        "diag_tiles": bell_draw(seeds[3], (ORDER, HALF_BAND), HALF_BAND ** -0.5, 0.5, ((0, 32),), jnp.float32),
        "upper_tiles": bell_draw(seeds[4], (ORDER, HALF_BAND), HALF_BAND ** -0.5, 0.5, ((0, 32),), jnp.float32),
    }


precise = lax.Precision.HIGHEST

def band_product(field, diag_tiles, upper_tiles):
    band_width = diag_tiles.shape[1]
    number = field.shape[0] // band_width
    field_tiles = field.reshape(number, band_width, field.shape[1])
    diagonal = diag_tiles.reshape(number, band_width, band_width)
    diagonal = 0.5 * (diagonal + jnp.swapaxes(diagonal, 1, 2))
    upper_part = upper_tiles.reshape(number, band_width, band_width)
    result = jnp.einsum('tij,tjm->tim', diagonal, field_tiles, precision=precise)
    forward = jnp.einsum('tij,tjm->tim', upper_part[:-1], field_tiles[1:], precision=precise)
    backward = jnp.einsum('tji,tjm->tim', upper_part[:-1], field_tiles[:-1], precision=precise)
    blank = jnp.zeros((1, band_width, field.shape[1]), jnp.float32)
    result = result + jnp.concatenate([forward, blank], 0) + jnp.concatenate([blank, backward], 0)
    return result.reshape(field.shape)

def to_half(values):
    return lax.optimization_barrier(values.astype(jnp.bfloat16)).astype(jnp.float32)

def node_filter(inverse, weight, current, couplings):
    parts = current.shape[0] // ROWS_DEV
    columns = current.shape[1]
    blocks = inverse.astype(jnp.float32).reshape(2, parts, ROWS_DEV, ROWS_DEV)
    vectors = current.astype(jnp.float32).reshape(parts, ROWS_DEV, columns)
    solved = jnp.einsum('cpij,pjm->cpim', blocks, vectors)
    first_tips = to_half(solved[:, :, :HALF_BAND])
    last_tips = to_half(solved[:, :, -HALF_BAND:])
    empty = jnp.zeros((2, 1, HALF_BAND, columns), jnp.float32)
    from_prior = jnp.concatenate([empty, last_tips[:, :-1]], 1)
    from_next = jnp.concatenate([first_tips[:, 1:], empty], 1)
    prior_coupling = jnp.concatenate([jnp.zeros((1, HALF_BAND, HALF_BAND), jnp.float32), couplings[:-1]], 0)
    edge_top = jnp.einsum('pji,cpjm->cpim', prior_coupling, from_prior, precision=precise)
    edge_bottom = jnp.einsum('pij,cpjm->cpim', couplings, from_next, precision=precise)
    edge_terms = to_half(jnp.concatenate([edge_top, edge_bottom], 2))
    corner = jnp.concatenate([blocks[..., :HALF_BAND], blocks[..., -HALF_BAND:]], 3)
    real_part = solved[0] + jnp.einsum('pij,pjm->pim', corner[0], edge_terms[0]) - jnp.einsum('pij,pjm->pim', corner[1], edge_terms[1])
    imag_part = solved[1] + jnp.einsum('pij,pjm->pim', corner[0], edge_terms[1]) + jnp.einsum('pij,pjm->pim', corner[1], edge_terms[0])
    return (weight[0] * real_part - weight[1] * imag_part).reshape(current.shape)

def reference(subspace, inverse, weights, diag_tiles, upper_tiles):
    order = subspace.shape[0]
    parts = order // ROWS_DEV
    couplings = upper_tiles.reshape(parts, ROWS_DEV, HALF_BAND)[:, -HALF_BAND:, :]
    current = subspace
    history = []
    orthonormal = jnp.zeros(subspace.shape, jnp.float32)
    for iteration in range(ITERS):

        def add_node(total, pair):
            return (total + node_filter(pair[0], pair[1], current, couplings), None)
        start = jnp.zeros(subspace.shape, jnp.float32)
        filtered, unused = lax.scan(add_node, start, (inverse, weights))
        gram_matrix = jnp.dot(filtered.T, filtered, precision=precise) / order
        factor = jnp.linalg.cholesky(gram_matrix)
        orthonormal = jax.scipy.linalg.solve_triangular(factor, filtered.T, lower=True).T
        imaged = band_product(orthonormal, diag_tiles, upper_tiles)
        history.append(jnp.dot(orthonormal.T, imaged, precision=precise) / order)
        current = orthonormal.astype(jnp.bfloat16)
    return (orthonormal, jnp.stack(history))
```

```python
import functools

import jax
import jax.numpy as jnp
from jax import lax
from jax.experimental import pallas as pl
from jax.experimental.pallas import tpu as pltpu
from jax.sharding import PartitionSpec as P

ITERS = 2
MESH = pl.DeviceIdType.MESH
F32, BF16 = jnp.float32, jnp.bfloat16
precise = lax.Precision.HIGHEST


def dot(a, b, ca=1, cb=0, precision=None):
    return lax.dot_general(
        a, b, (((ca,), (cb,)), ((), ())), precision=precision, preferred_element_type=F32
    )


def split3(x):
    high = x.astype(BF16)
    rest = x - high.astype(F32)
    middle = rest.astype(BF16)
    low = (rest - middle.astype(F32)).astype(BF16)
    return high, middle, low


def panel_step(a, k, size):
    r0 = 8 * k
    half, lane0 = r0 // 128, r0 % 128
    halves = size // 128
    row = [[a[h, pl.ds(r0 + i, 8, stride=0), :] for h in range(halves)] for i in range(8)]
    e = [
        [jnp.broadcast_to(row[i][half][:, lane0 + j : lane0 + j + 1], (8, 128)) for j in range(i + 1)]
        for i in range(8)
    ]
    t = [[None] * 8 for _ in range(8)]
    for j in range(8):
        r = lax.rsqrt(e[j][j])
        for q in range(j):
            t[j][q] = t[j][q] * r
        t[j][j] = r
        m = {i: e[i][j] * r for i in range(j + 1, 8)}
        for i in range(j + 1, 8):
            for q in range(j + 1, i + 1):
                e[i][q] = e[i][q] - m[i] * m[q]
            for q in range(j + 1):
                prev = t[i][q]
                t[i][q] = -m[i] * t[j][q] if prev is None else prev - m[i] * t[j][q]
    sub = lax.broadcasted_iota(jnp.int32, (8, 128), 0)
    lane = lax.broadcasted_iota(jnp.int32, (8, 128), 1)
    out = [jnp.zeros((8, 128), F32) for _ in range(halves)]
    diag = jnp.zeros((8, 128), F32)
    for q in range(8):
        col = jnp.zeros((8, 128), F32)
        for i in range(q, 8):
            col = jnp.where(sub == i, t[i][q], col)
        for h in range(halves):
            out[h] = out[h] + col * row[q][h]
        diag = jnp.where(lane == lane0 + q, col, diag)
    inside = (lane >= lane0) & (lane < lane0 + 8)
    new = [jnp.where(inside, diag, out[h]) if h == half else out[h] for h in range(halves)]
    for h in range(halves):
        a[h, r0 : r0 + 8, :] = new[h]
    if r0 + 8 >= size:
        return
    below = size - r0 - 8
    base = 128 * ((r0 + 8) // 128)
    lh, lm, ll = split3(jnp.concatenate([out[h] for h in range(base // 128, halves)], axis=1))
    rh, rm, rl = split3(jnp.concatenate(new, axis=1))
    left = jnp.concatenate([lh, lh, lm, lh, ll, lm], axis=0)
    right = jnp.concatenate([rh, rm, rh, rl, rh, rm], axis=0)
    update = dot(left, right, 0, 0)
    off = r0 + 8 - base
    for h in range(halves):
        old = a[h, r0 + 8 : size, :]
        if h == half:
            lanes = lax.broadcasted_iota(jnp.int32, (below, 128), 1)
            old = jnp.where((lanes >= lane0) & (lanes < lane0 + 8), 0.0, old)
        a[h, r0 + 8 : size, :] = old - update[off:, 128 * h : 128 * h + 128]


def inverse_factor(gram, a, scale):
    size = gram.shape[0]
    halves = size // 128
    for h in range(halves):
        a[h] = gram[:, 128 * h : 128 * h + 128] * scale
    for k in range(size // 8):
        panel_step(a, k, size)
    rows = lax.broadcasted_iota(jnp.int32, (size, size), 0)
    columns = lax.broadcasted_iota(jnp.int32, (size, size), 1)
    return jnp.where(rows >= columns, jnp.concatenate([a[h] for h in range(halves)], axis=1), 0.0)


def dense_kernel(scale, gram, half_projected, field, out, current, projected, a):
    inverse = inverse_factor(gram[...], a, scale)
    tile = 128
    for t in range(field.shape[0] // tile):
        rows = pl.ds(t * tile, tile)
        value = dot(field[rows, :], inverse, 1, 1, precise)
        out[rows, :] = value
        current[rows, :] = value.astype(BF16)
    left = dot(inverse, half_projected[...] * scale, 1, 0, precise)
    q = dot(left, inverse, 1, 1, precise)
    projected[...] = q + q.T


def dense_part(gram, half_projected, field, order):
    rows, columns = field.shape
    whole = pl.BlockSpec(memory_space=pltpu.VMEM)
    return pl.pallas_call(
        functools.partial(dense_kernel, 1.0 / order),
        out_shape=(
            jax.ShapeDtypeStruct((rows, columns), F32),
            jax.ShapeDtypeStruct((rows, columns), BF16),
            jax.ShapeDtypeStruct((columns, columns), F32),
        ),
        in_specs=[whole] * 3,
        out_specs=(whole,) * 3,
        scratch_shapes=[pltpu.VMEM((columns // 128, columns, 128), F32)],
    )(gram, half_projected, field)


def filter_kernel(
    nodes, parts, current, inverse, weights, diag, upper, field_out, gram_out, half_out,
    firsts, ups, from_next, from_prior, term, arrived, field, next_rows,
    gram, gram_pair, gram_z, gram_all, half, half_pair, half_z, half_all,
    tip_send, tip_recv, rs_send, rs_recv, ag_send, ag_recv, row_send, row_recv,
    pair_send, pair_recv, z_send, z_recv, all_send, all_recv,
):
    j, p = lax.axis_index("node"), lax.axis_index("rows")
    core = lax.rem(p, 2)
    sibling = p + 1 - 2 * core
    up, down = lax.rem(p + 1, parts), lax.rem(p + parts - 1, parts)
    cross = lax.rem(p + parts - 1 + 2 * core, parts)
    chips = parts // 2
    z = p // 2
    size, columns = current.shape
    band = diag.shape[1]
    chunk = size // nodes

    def node_at(k):
        return lax.rem(j + k, nodes)

    def part_at(k):
        return lax.rem(p + 2 * k, parts)

    barrier = pltpu.get_barrier_semaphore()

    def greet(device):
        pl.semaphore_signal(barrier, inc=1, device_id=device, device_id_type=MESH)

    greet((j, cross))
    greet((j, sibling))
    lax.fori_loop(1, nodes, lambda k, _: (greet((node_at(k), p)), greet((node_at(k), sibling)), 0)[-1], 0)
    lax.fori_loop(1, chips, lambda k, _: (greet((j, part_at(k))), 0)[-1], 0)

    def copy(src, dst, send, recv, device):
        return pltpu.make_async_remote_copy(
            src_ref=src, dst_ref=dst, send_sem=send, recv_sem=recv, device_id=device, device_id_type=MESH
        )

    coupling = upper[size - band :, :]
    for part in range(2):
        firsts[part] = dot(inverse[part, :band, :], current[...]).astype(BF16)
        last = dot(inverse[part, size - band :, :], current[...]).astype(BF16).astype(F32)
        ups[part] = dot(coupling, last, 0, 0, precise).astype(BF16)
    pl.semaphore_wait(barrier, 2 * nodes - 1 + chips - 1 + 1)
    to_down = copy(firsts, from_next, tip_send.at[0], tip_recv.at[0], (j, down))
    to_up = copy(ups, from_prior, tip_send.at[1], tip_recv.at[1], (j, up))
    to_down.start()
    to_up.start()

    w0, w1 = weights[0, 0], weights[0, 1]
    groups = 4
    tile = size // groups
    for t in range(groups):
        rows = pl.ds(t * tile, tile)
        term[rows, :] = w0 * dot(inverse[0, rows, :], current[...]) - w1 * dot(inverse[1, rows, :], current[...])

    to_down.wait()
    to_up.wait()
    top, bottom = [], []
    for part in range(2):
        below = dot(coupling, from_next[part].astype(F32), 1, 0, precise)
        top.append(jnp.where(p == 0, 0.0, from_prior[part].astype(F32)).astype(BF16))
        bottom.append(jnp.where(p == parts - 1, 0.0, below).astype(BF16))
    top, bottom = jnp.concatenate(top, axis=1), jnp.concatenate(bottom, axis=1)

    def rs_copy(k):
        to = node_at(k)
        rows = pl.ds(pl.multiple_of(to * chunk, 8), chunk)
        return copy(term.at[rows, :], arrived.at[j], rs_send.at[to], rs_recv.at[j], (to, p))

    def rs_send_one(to):
        rows = pl.ds(pl.multiple_of(to * chunk, 8), chunk)

        @pl.when(to != j)
        def _():
            copy(term.at[rows, :], arrived.at[j], rs_send.at[to], rs_recv.at[j], (to, p)).start()

    per_group = nodes // groups

    def node_group(t, _):
        g = lax.rem(t + j // per_group, groups)
        rows = pl.ds(pl.multiple_of(g * tile, 8), tile)
        real = dot(inverse[0, rows, :band], top) + dot(inverse[0, rows, size - band :], bottom)
        imag = dot(inverse[1, rows, :band], top) + dot(inverse[1, rows, size - band :], bottom)
        change = w0 * (real[:, :columns] - imag[:, columns:]) - w1 * (real[:, columns:] + imag[:, :columns])
        term[rows, :] = term[rows, :] + change
        for k in range(per_group):
            rs_send_one(g * per_group + lax.rem(j + k, per_group))
        return 0

    lax.fori_loop(0, groups, node_group, 0)
    own = pl.ds(pl.multiple_of(j * chunk, 8), chunk)

    def add_one(k, total):
        source = node_at(nodes - k)
        copy(term.at[own, :], arrived.at[source], rs_send.at[source], rs_recv.at[source], (source, p)).wait_recv()
        return total + arrived[source]

    field[own, :] = lax.fori_loop(1, nodes, add_one, term[own, :])

    def ag_copy(to, source):
        rows = pl.ds(pl.multiple_of(source * chunk, 8), chunk)
        return copy(field.at[rows, :], field.at[rows, :], ag_send.at[to], ag_recv.at[source], (to, p))

    def ag_start(k, _):
        ag_copy(node_at(k), j).start()
        return 0

    lax.fori_loop(1, nodes, ag_start, 0)

    def ag_wait(k, _):
        source = node_at(nodes - k)
        ag_copy(source, source).wait_recv()
        return 0

    lax.fori_loop(1, nodes, ag_wait, 0)
    to_prior = copy(field.at[pl.ds(0, band), :], next_rows, row_send, row_recv, (j, down))
    to_prior.start()

    share = columns // nodes // 2

    def rows_of(node, which):
        return pl.ds(pl.multiple_of((node * 2 + which) * share, 8), share)

    def pair_copy(m, source, target):
        return copy(source.at[rows_of(j, 1 - core), :], target, pair_send.at[m], pair_recv.at[m], (j, sibling))

    def z_copy(m, target, source, to):
        return copy(target.at[source], target.at[source], z_send.at[m, to // 2], z_recv.at[m, source], (j, to))

    def z_start(m, source, pair, target):
        pair_copy(m, source, pair).wait()
        target[z] = source[rows_of(j, core), :] + pair[...]
        lax.fori_loop(1, chips, lambda k, _: (z_copy(m, target, z, part_at(k)).start(), 0)[-1], 0)

    def all_copy(m, target, node, which, to_node, to_which):
        rows = rows_of(node, which)
        to = (to_node, p - core + to_which)
        return copy(target.at[rows, :], target.at[rows, :], all_send.at[m, to_node * 2 + to_which], all_recv.at[m, node * 2 + which], to)

    def all_start(m, target, result):
        def add(k, total):
            source = lax.rem(z + chips - k, chips)
            z_copy(m, target, source, part_at(k)).wait_recv()
            return total + target[source]

        result[rows_of(j, core), :] = lax.fori_loop(1, chips, add, target[z])
        all_copy(m, result, j, core, j, 1 - core).start()

        def send(k, _):
            all_copy(m, result, j, core, node_at(k), core).start()
            all_copy(m, result, j, core, node_at(k), 1 - core).start()
            return 0

        lax.fori_loop(1, nodes, send, 0)

    def all_wait(m, result):
        all_copy(m, result, j, 1 - core, j, 1 - core).wait_recv()

        def wait(k, _):
            all_copy(m, result, node_at(k), core, node_at(k), core).wait_recv()
            all_copy(m, result, node_at(k), 1 - core, node_at(k), 1 - core).wait_recv()
            return 0

        lax.fori_loop(1, nodes, wait, 0)

    gram[...] = dot(field[...], field[...], 0, 0, precise)
    pair_copy(0, gram, gram_pair).start()
    z_start(0, gram, gram_pair, gram_z)

    to_prior.wait()
    tiles = size // band
    total = jnp.zeros((columns, columns), F32)
    for t in range(tiles):
        rows = pl.ds(t * band, band)
        after = jnp.where(p == parts - 1, 0.0, next_rows[...]) if t == tiles - 1 else field[pl.ds((t + 1) * band, band), :]
        imaged = dot(0.5 * diag[rows, :], field[rows, :], 1, 0, precise) + dot(upper[rows, :], after, 1, 0, precise)
        total = total + dot(field[rows, :], imaged, 0, 0, precise)
    half[...] = total
    pair_copy(1, half, half_pair).start()
    z_start(1, half, half_pair, half_z)

    all_start(0, gram_z, gram_all)
    all_start(1, half_z, half_all)
    field_out[...] = field[...]
    all_wait(0, gram_all)
    gram_out[...] = gram_all[...]
    all_wait(1, half_all)
    half_out[...] = half_all[...]

    def drain(k, _):
        to = node_at(k)
        rs_copy(k).wait_send()
        ag_copy(to, j).wait_send()
        for m, target in ((0, gram_all), (1, half_all)):
            all_copy(m, target, j, core, to, core).wait_send()
            all_copy(m, target, j, core, to, 1 - core).wait_send()
        return 0

    lax.fori_loop(1, nodes, drain, 0)

    def drain_z(k, _):
        for m, target in ((0, gram_z), (1, half_z)):
            z_copy(m, target, z, part_at(k)).wait_send()
        return 0

    lax.fori_loop(1, chips, drain_z, 0)
    for m, target in ((0, gram_all), (1, half_all)):
        all_copy(m, target, j, core, j, 1 - core).wait_send()


def filter_part(current, inverse, weights, diag, upper, nodes, parts, number):
    rows, columns = current.shape
    band = diag.shape[1]
    chunk = rows // nodes
    share = columns // nodes // 2
    whole = pl.BlockSpec(memory_space=pltpu.VMEM)
    square = (columns, columns)
    sums = [
        pltpu.VMEM(square, F32),
        pltpu.VMEM((share, columns), F32),
        pltpu.VMEM((parts // 2, share, columns), F32),
        pltpu.VMEM(square, F32),
    ]
    dma = pltpu.SemaphoreType.DMA
    return pl.pallas_call(
        functools.partial(filter_kernel, nodes, parts),
        out_shape=(
            jax.ShapeDtypeStruct((rows, columns), F32),
            jax.ShapeDtypeStruct(square, F32),
            jax.ShapeDtypeStruct(square, F32),
        ),
        in_specs=[whole, whole, pl.BlockSpec(memory_space=pltpu.SMEM), whole, whole],
        out_specs=(whole,) * 3,
        scratch_shapes=[pltpu.VMEM((2, band, columns), BF16)] * 4
        + [
            pltpu.VMEM((rows, columns), F32),
            pltpu.VMEM((nodes, chunk, columns), F32),
            pltpu.VMEM((rows, columns), F32),
            pltpu.VMEM((band, columns), F32),
        ]
        + sums * 2
        + [dma((2,)), dma((2,))]
        + [dma((nodes,))] * 4
        + [dma(()), dma(())]
        + [dma((2,)), dma((2,))]
        + [dma((2, parts // 2))] * 2
        + [dma((2, 2 * nodes))] * 2,
        compiler_params=pltpu.CompilerParams(
            collective_id=number, has_side_effects=True, vmem_limit_bytes=48 * 1024 * 1024
        ),
    )(current, inverse[0], weights, diag, upper)


def per_device(subspace, inverse, weights, diag_tiles, upper_tiles):
    nodes, parts = lax.axis_size("node"), lax.axis_size("rows")
    order = subspace.shape[0] * parts
    current, history = subspace, []
    for iteration in range(ITERS):
        field, gram, half = filter_part(
            current, inverse, weights, diag_tiles, upper_tiles, nodes, parts, iteration
        )
        orthonormal, current, projected = dense_part(gram, half, field, order)
        history.append(projected)
    return (orthonormal, jnp.stack(history))


def solution(mesh):
    placed = (
        P("rows", None),
        P("node", None, "rows", None),
        P("node", None),
        P("rows", None),
        P("rows", None),
    )
    return jax.shard_map(
        per_device, mesh=mesh, in_specs=placed, out_specs=(P("rows", None), P()), check_vma=False
    )
```

```python
import functools

import jax
import jax.numpy as jnp
from jax import lax
from jax.experimental import pallas as pl
from jax.experimental.pallas import tpu as pltpu
from jax.sharding import PartitionSpec as P

ITERS = 2
MESH = pl.DeviceIdType.MESH
F32, BF16 = jnp.float32, jnp.bfloat16
precise = lax.Precision.HIGHEST


def dot(a, b, ca=1, cb=0, precision=None):
    return lax.dot_general(
        a, b, (((ca,), (cb,)), ((), ())), precision=precision, preferred_element_type=F32
    )


def split3(x):
    high = x.astype(BF16)
    rest = x - high.astype(F32)
    middle = rest.astype(BF16)
    low = (rest - middle.astype(F32)).astype(BF16)
    return high, middle, low


def panel_step(a, k, size):
    r0 = 8 * k
    half, lane0 = r0 // 128, r0 % 128
    halves = size // 128
    row = [[jnp.broadcast_to(a[h, r0 + i : r0 + i + 1, :], (8, 128)) for h in range(halves)] for i in range(8)]
    e = [
        [jnp.broadcast_to(row[i][half][:, lane0 + j : lane0 + j + 1], (8, 128)) for j in range(i + 1)]
        for i in range(8)
    ]
    t = [[None] * 8 for _ in range(8)]
    for j in range(8):
        r = lax.rsqrt(e[j][j])
        for q in range(j):
            t[j][q] = t[j][q] * r
        t[j][j] = r
        m = {i: e[i][j] * r for i in range(j + 1, 8)}
        for i in range(j + 1, 8):
            for q in range(j + 1, i + 1):
                e[i][q] = e[i][q] - m[i] * m[q]
            for q in range(j + 1):
                prev = t[i][q]
                t[i][q] = -m[i] * t[j][q] if prev is None else prev - m[i] * t[j][q]
    sub = lax.broadcasted_iota(jnp.int32, (8, 128), 0)
    lane = lax.broadcasted_iota(jnp.int32, (8, 128), 1)
    out = [jnp.zeros((8, 128), F32) for _ in range(halves)]
    diag = jnp.zeros((8, 128), F32)
    for q in range(8):
        col = jnp.zeros((8, 128), F32)
        for i in range(q, 8):
            col = jnp.where(sub == i, t[i][q], col)
        for h in range(halves):
            out[h] = out[h] + col * row[q][h]
        diag = jnp.where(lane == lane0 + q, col, diag)
    inside = (lane >= lane0) & (lane < lane0 + 8)
    new = [jnp.where(inside, diag, out[h]) if h == half else out[h] for h in range(halves)]
    for h in range(halves):
        a[h, r0 : r0 + 8, :] = new[h]
    if r0 + 8 >= size:
        return
    below = size - r0 - 8
    base = 128 * ((r0 + 8) // 128)
    lh, lm, ll = split3(jnp.concatenate([out[h] for h in range(base // 128, halves)], axis=1))
    rh, rm, rl = split3(jnp.concatenate(new, axis=1))
    left = jnp.concatenate([lh, lh, lm, lh, ll, lm], axis=0)
    right = jnp.concatenate([rh, rm, rh, rl, rh, rm], axis=0)
    update = dot(left, right, 0, 0)
    off = r0 + 8 - base
    for h in range(halves):
        old = a[h, r0 + 8 : size, :]
        if h == half:
            lanes = lax.broadcasted_iota(jnp.int32, (below, 128), 1)
            old = jnp.where((lanes >= lane0) & (lanes < lane0 + 8), 0.0, old)
        a[h, r0 + 8 : size, :] = old - update[off:, 128 * h : 128 * h + 128]


def packed(whole):
    half = whole.shape[0] // 2
    rows = lax.broadcasted_iota(jnp.int32, (half, half), 0)
    columns = lax.broadcasted_iota(jnp.int32, (half, half), 1)
    last = whole[half:, half:]
    row = jnp.sum(jnp.where(rows == columns, last, 0.0), axis=0, keepdims=True)
    return jnp.where(rows <= columns, whole[:half, :half], last), whole[:half, half:], row


def unpacked(first, second, row):
    half = first.shape[0]
    rows = lax.broadcasted_iota(jnp.int32, (half, half), 0)
    columns = lax.broadcasted_iota(jnp.int32, (half, half), 1)
    turned = first.T
    last = jnp.where(rows > columns, first, jnp.where(rows < columns, turned, row))
    return jnp.where(rows <= columns, first, turned), second, last


def kernel(
    nodes, parts, scale,
    subspace, inverse, weights, diag_in, upper_in, out, projected,
    current, blocks, diag, upper, firsts, ups, from_next, from_prior, edge,
    term, ra, rb, pa, pb, qa, qb, field, next_rows, imaged,
    block, mine, pair, pk, grs, zb, res, rest, a, inv, ortho, proj,
    load, tip_send, tip_recv, rsa_send, rsa_recv, rsb_send, rsb_recv,
    rsc_send, rsc_recv, rsd_send, rsd_recv,
    aga_send, aga_recv, agb_send, agb_recv, agc_send, agc_recv, agd_send, agd_recv,
    row_send, row_recv, pair_send, pair_recv, grs_send, grs_recv,
    z_send, z_recv, all_send, all_recv, fin_send, fin_recv,
):
    j, p = lax.axis_index("node"), lax.axis_index("rows")
    side = int(round(nodes**0.5))
    x, y = j // side, lax.rem(j, side)
    core = lax.rem(p, 2)
    sibling = p + 1 - 2 * core
    up, down = lax.rem(p + 1, parts), lax.rem(p + parts - 1, parts)
    cross = lax.rem(p + parts - 1 + 2 * core, parts)
    chips = parts // 2
    z = p // 2
    size, columns = current.shape
    band = diag.shape[1]
    piece = size // nodes // 2
    half = columns // 2
    share = half // nodes

    def each(start, stop, act):
        def step(k, carry):
            act(k)
            return carry

        lax.fori_loop(start, stop, step, 0)

    def turn(value, k, count):
        return lax.rem(value + k, count)

    def copy(src, dst, send, recv, device):
        return pltpu.make_async_remote_copy(
            src_ref=src, dst_ref=dst, send_sem=send, recv_sem=recv, device_id=device, device_id_type=MESH
        )

    loads = [
        pltpu.make_async_copy(subspace, current, load.at[0]),
        pltpu.make_async_copy(inverse, blocks, load.at[1]),
        pltpu.make_async_copy(upper_in, upper, load.at[2]),
        pltpu.make_async_copy(diag_in, diag, load.at[3]),
    ]
    for item in loads:
        item.start()
    barrier = pltpu.get_barrier_semaphore()

    def greet(device):
        pl.semaphore_signal(barrier, inc=1, device_id=device, device_id_type=MESH)

    each(1, chips, lambda k: greet((j, turn(p, 2 * k, parts))))
    each(1, nodes, lambda k: greet((turn(j, k, nodes), p)))
    greet((j, cross))
    greet((j, sibling))
    for item in loads:
        item.wait()
    w0, w1 = weights[0, 0], weights[0, 1]

    def tips():
        coupling = upper[size - band :, :]
        for part in range(2):
            last = dot(blocks[part, size - band :, :], current[...]).astype(BF16).astype(F32)
            ups[part] = dot(coupling, last, 0, 0, precise).astype(BF16)
            firsts[part] = dot(blocks[part, :band, :], current[...]).astype(BF16)

    tips()
    pl.semaphore_wait(barrier, nodes - 1 + chips - 1 + 2)

    def pair_copy(it, m):
        return copy(block.at[m], pair.at[it, m], pair_send.at[it, m], pair_recv.at[it, m], (j, sibling))

    def pack_start(it, m, whole):
        first, second, row = packed(whole)
        mine[m] = jnp.where(core == 0, first, second)
        block[m, :half, :] = jnp.where(core == 0, second, first)
        block[m, half:, :] = jnp.broadcast_to(row, (8, half))
        pair_copy(it, m).start()

    def pack_sum(it, m):
        pair_copy(it, m).wait()
        total = mine[m] + pair[it, m, :half, :]
        pk[m, :, :share, :] = total.reshape(nodes, share, half)
        row = block[m, half:, :] + pair[it, m, half:, :]
        pk[m, :, share:, :] = jnp.broadcast_to(row[None], (nodes, 8, half))

    slice_rows = pl.ds(0, share + 1)

    def grs_copy(it, source, to):
        return copy(
            pk.at[0, to, slice_rows, :], grs.at[it, source, slice_rows, :],
            grs_send.at[it, to], grs_recv.at[it, source], (to, p),
        )

    def z_copy(it, m, source, to):
        here = zb.at[it, m, source, slice_rows, :]
        return copy(here, here, z_send.at[it, m, to], z_recv.at[it, m, source], (j, 2 * to + core))

    def z_start(it, m, value):
        zb[it, m, z, slice_rows, :] = value
        each(1, chips, lambda k: z_copy(it, m, z, turn(z, k, chips)).start())

    def all_copy(it, m, source, to):
        here = res.at[it, m, core, pl.ds(pl.multiple_of(source * share, 8), share), :]
        return copy(here, here, all_send.at[it, m, to], all_recv.at[it, m, source], (to, p))

    def z_finish(it, m):
        def add(k, total):
            source = turn(z, chips - k, chips)
            z_copy(it, m, source, source).wait_recv()
            return total + zb[it, m, source, slice_rows, :]

        total = lax.fori_loop(1, chips, add, zb[it, m, z, slice_rows, :])
        rest[it, m] = jnp.broadcast_to(total[share : share + 1, :], (8, half))
        res[it, m, core, pl.ds(pl.multiple_of(j * share, 8), share), :] = total[:share, :]
        each(1, nodes, lambda k: all_copy(it, m, j, turn(j, k, nodes)).start())

    def fin_copy(it, m, which):
        here = res.at[it, m, which]
        return copy(here, here, fin_send.at[it, m], fin_recv.at[it, m], (j, sibling))

    def all_finish(it, m):
        def wait(k):
            source = turn(j, nodes - k, nodes)
            all_copy(it, m, source, source).wait_recv()

        each(1, nodes, wait)
        fin_copy(it, m, core).start()

    def summed(it, m):
        fin_copy(it, m, 1 - core).wait_recv()
        return unpacked(res[it, m, 0], res[it, m, 1], rest[it, m, 0:1, :])

    def project(it):
        first, second, last = summed(it, 1)
        whole = jnp.concatenate(
            [jnp.concatenate([first, second], axis=1), jnp.concatenate([second.T, last], axis=1)], axis=0
        )
        left = dot(inv[it], whole * scale, 1, 0, precise)
        proj[it] = dot(left, inv[it], 1, 1, precise)

    def drained(it):
        tip_down, tip_up = tip_copies(it)
        tip_down.wait_send()
        tip_up.wait_send()
        row_copy(it).wait_send()

        def over_side(k):
            xx, yy = turn(x, k, side), turn(y, k, side)
            rsa_copy(it, xx, x).wait_send()
            rsc_copy(it, yy, y).wait_send()
            rsd_copy(it, xx, x).wait_send()
            aga_copy(it, xx, x).wait_send()
            agb_copy(it, yy, y).wait_send()
            agc_copy(it, yy, y).wait_send()
            agd_copy(it, xx, x).wait_send()
            each(0, side, lambda g: rsb_copy(it, g, yy, y).wait_send())

        each(1, side, over_side)

        def over_nodes(k):
            to = turn(j, k, nodes)
            grs_copy(it, j, to).wait_send()
            all_copy(it, 0, j, to).wait_send()

        each(1, nodes, over_nodes)
        each(1, chips, lambda k: z_copy(it, 0, z, turn(z, k, chips)).wait_send())
        each(1, chips, lambda k: z_copy(it, 1, z, turn(z, k, chips)).wait_send())
        fin_copy(it, 0, core).wait_send()

    def projected_drained(it):
        each(1, nodes, lambda k: all_copy(it, 1, j, turn(j, k, nodes)).wait_send())
        fin_copy(it, 1, core).wait_send()

    def tip_copies(it):
        return (
            copy(firsts, from_next.at[it], tip_send.at[it, 0], tip_recv.at[it, 0], (j, down)),
            copy(ups, from_prior.at[it], tip_send.at[it, 1], tip_recv.at[it, 1], (j, up)),
        )

    def rsa_copy(it, g, source):
        return copy(term.at[g, :, 0], ra.at[it, source], rsa_send.at[it, g], rsa_recv.at[it, source], (g * side + y, p))

    def rsb_copy(it, g, to, source):
        return copy(
            term.at[g, to, 1], rb.at[it, source, g], rsb_send.at[it, to, g], rsb_recv.at[it, source, g], (x * side + to, p)
        )

    def rsc_copy(it, to, source):
        return copy(pa.at[to], qa.at[it, source], rsc_send.at[it, to], rsc_recv.at[it, source], (x * side + to, p))

    def rsd_copy(it, to, source):
        return copy(pb.at[to], qb.at[it, source], rsd_send.at[it, to], rsd_recv.at[it, source], (to * side + y, p))

    def aga_copy(it, to, source):
        here = field.at[it, source, y, 0]
        return copy(here, here, aga_send.at[it, to], aga_recv.at[it, source], (to * side + y, p))

    def agb_copy(it, to, source):
        here = field.at[it, x, source, 1]
        return copy(here, here, agb_send.at[it, to], agb_recv.at[it, source], (x * side + to, p))

    def agc_copy(it, to, source):
        here = field.at[it, :, source, 0]
        return copy(here, here, agc_send.at[it, to], agc_recv.at[it, source], (x * side + to, p))

    def agd_copy(it, to, source):
        here = field.at[it, source, :, 1]
        return copy(here, here, agd_send.at[it, to], agd_recv.at[it, source], (to * side + y, p))

    def row_copy(it):
        return copy(edge, next_rows.at[it], row_send.at[it], row_recv.at[it], (j, down))

    tile = size // side

    def iteration(it, carry):
        tip_down, tip_up = tip_copies(it)
        tip_up.start()
        tip_down.start()
        for g in range(side):
            rows = pl.ds(g * tile, tile)
            value = w0 * dot(blocks[0, rows, :], current[...]) - w1 * dot(blocks[1, rows, :], current[...])
            term[g] = value.reshape(side, 2, piece, columns)

        @pl.when(it > 0)
        def _():
            all_finish(it - 1, 1)
            project(it - 1)
            projected_drained(it - 1)

        tip_down.wait_recv()
        coupling = upper[size - band :, :]
        bottom = []
        for part in range(2):
            below = dot(coupling, from_next[it, part].astype(F32), 1, 0, precise)
            bottom.append(jnp.where(p == parts - 1, 0.0, below).astype(BF16))
        tip_up.wait_recv()
        top = [jnp.where(p == 0, 0.0, from_prior[it, part].astype(F32)).astype(BF16) for part in range(2)]
        top, bottom = jnp.concatenate(top, axis=1), jnp.concatenate(bottom, axis=1)

        def group(t):
            g = turn(x, t + 1, side)
            rows = pl.ds(pl.multiple_of(g * tile, 8), tile)
            real = dot(blocks[0, rows, :band], top) + dot(blocks[0, rows, size - band :], bottom)
            imag = dot(blocks[1, rows, :band], top) + dot(blocks[1, rows, size - band :], bottom)
            change = w0 * (real[:, :columns] - imag[:, columns:]) - w1 * (real[:, columns:] + imag[:, :columns])
            term[g] = term[g] + change.reshape(side, 2, piece, columns)

            @pl.when(g != x)
            def _():
                rsa_copy(it, g, x).start()

            each(1, side, lambda k: rsb_copy(it, g, turn(y, k, side), y).start())

        each(0, side, group)

        def add_a(k, total):
            source = turn(x, side - k, side)
            rsa_copy(it, source, source).wait_recv()
            return total + ra[it, source]

        pa[...] = lax.fori_loop(1, side, add_a, term[x, :, 0])
        each(1, side, lambda k: rsc_copy(it, turn(y, k, side), y).start())

        def add_b(k, total):
            source = turn(y, side - k, side)
            each(0, side, lambda g: rsb_copy(it, g, source, source).wait_recv())
            return total + rb[it, source]

        pb[...] = lax.fori_loop(1, side, add_b, term[:, y, 1])
        each(1, side, lambda k: rsd_copy(it, turn(x, k, side), x).start())

        def add_c(k, total):
            source = turn(y, side - k, side)
            rsc_copy(it, source, source).wait_recv()
            return total + qa[it, source]

        field[it, x, y, 0] = lax.fori_loop(1, side, add_c, pa[y])

        def add_d(k, total):
            source = turn(x, side - k, side)
            rsd_copy(it, source, source).wait_recv()
            return total + qb[it, source]

        field[it, x, y, 1] = lax.fori_loop(1, side, add_d, pb[x])

        own = field[it, x, y].reshape(2 * piece, columns)
        pack_start(it, 0, dot(own, own, 0, 0, precise))
        pack_sum(it, 0)
        each(1, nodes, lambda k: grs_copy(it, j, turn(j, k, nodes)).start())

        def add_g(k, total):
            source = turn(j, nodes - k, nodes)
            grs_copy(it, source, source).wait_recv()
            return total + grs[it, source, slice_rows, :]

        z_start(it, 0, lax.fori_loop(1, nodes, add_g, pk[0, j, slice_rows, :]))

        def ag_first(k):
            aga_copy(it, turn(x, k, side), x).start()
            agb_copy(it, turn(y, k, side), y).start()

        each(1, side, ag_first)

        def ag_first_wait(k):
            aga_copy(it, turn(x, k, side), turn(x, k, side)).wait_recv()

        each(1, side, ag_first_wait)
        each(1, side, lambda k: agc_copy(it, turn(y, k, side), y).start())

        def ag_second_wait(k):
            agb_copy(it, turn(y, k, side), turn(y, k, side)).wait_recv()

        each(1, side, ag_second_wait)
        each(1, side, lambda k: agd_copy(it, turn(x, k, side), x).start())
        z_finish(it, 0)

        def ag_last_wait(k):
            agc_copy(it, turn(y, k, side), turn(y, k, side)).wait_recv()
            agd_copy(it, turn(x, k, side), turn(x, k, side)).wait_recv()

        each(1, side, ag_last_wait)
        whole = field[it].reshape(size, columns)
        edge[...] = whole[:band, :]
        row_copy(it).start()
        tiles = size // band
        for t in range(tiles - 1):
            rows = slice(t * band, t * band + band)
            imaged[rows, :] = dot(0.5 * diag[rows, :], whole[rows, :], 1, 0, precise) + dot(
                upper[rows, :], whole[t * band + band : t * band + 2 * band, :], 1, 0, precise
            )
        rows = slice(size - band, size)
        near = dot(0.5 * diag[rows, :], whole[rows, :], 1, 0, precise)
        row_copy(it).wait_recv()
        after = jnp.where(p == parts - 1, 0.0, next_rows[it])
        imaged[rows, :] = near + dot(upper[rows, :], after, 1, 0, precise)
        product = dot(whole, imaged[...], 0, 0, precise)
        pack_start(it, 1, product + product.T)

        all_finish(it, 0)
        pack_sum(it, 1)
        z_start(it, 1, pk[1, j, slice_rows, :])
        first, second, last = summed(it, 0)
        a[0, :half, :] = first * scale
        a[1, :half, :] = second * scale
        a[0, half:, :] = jnp.zeros((half, half), F32)
        a[1, half:, :] = last * scale
        steps = columns // 8
        for k in range(steps):
            if k == (5 * steps) // 8:
                z_finish(it, 1)
            panel_step(a, k, columns)
        rows = lax.broadcasted_iota(jnp.int32, (columns, columns), 0)
        cols = lax.broadcasted_iota(jnp.int32, (columns, columns), 1)
        factor = jnp.where(rows >= cols, jnp.concatenate([a[0], a[1]], axis=1), 0.0)
        inv[it] = factor
        for g in range(side):
            rows = pl.ds(g * tile, tile)
            value = dot(field[it, g].reshape(tile, columns), factor, 1, 1, precise)
            ortho[rows, :] = value
            current[rows, :] = value.astype(BF16)
        drained(it)

        @pl.when(it < ITERS - 1)
        def _():
            tips()

        return carry

    lax.fori_loop(0, ITERS, iteration, 0)
    store = pltpu.make_async_copy(ortho, out, load.at[0])
    store.start()
    all_finish(ITERS - 1, 1)
    project(ITERS - 1)
    projected_drained(ITERS - 1)
    last_store = pltpu.make_async_copy(proj, projected, load.at[1])
    last_store.start()
    store.wait()
    last_store.wait()


def per_device(subspace, inverse, weights, diag_tiles, upper_tiles):
    nodes, parts = lax.axis_size("node"), lax.axis_size("rows")
    rows, columns = subspace.shape
    band = diag_tiles.shape[1]
    side = int(round(nodes**0.5))
    piece = rows // nodes // 2
    half = columns // 2
    share = half // nodes
    chips = parts // 2
    n = ITERS
    vmem, dma = pltpu.VMEM, pltpu.SemaphoreType.DMA
    anywhere = pl.BlockSpec(memory_space=pl.ANY)
    tip = (2, band, columns)
    scratch = [
        vmem((rows, columns), BF16), vmem((2, rows, rows), BF16), vmem((rows, band), F32), vmem((rows, band), F32),
        vmem(tip, BF16), vmem(tip, BF16), vmem((n, *tip), BF16), vmem((n, *tip), BF16), vmem((band, columns), F32),
        vmem((side, side, 2, piece, columns), F32),
        vmem((n, side, side, piece, columns), F32), vmem((n, side, side, piece, columns), F32),
        vmem((side, piece, columns), F32), vmem((side, piece, columns), F32),
        vmem((n, side, piece, columns), F32), vmem((n, side, piece, columns), F32),
        vmem((n, side, side, 2, piece, columns), F32), vmem((n, band, columns), F32), vmem((rows, columns), F32),
        vmem((2, half + 8, half), F32), vmem((2, half, half), F32), vmem((n, 2, half + 8, half), F32),
        vmem((2, nodes, share + 8, half), F32), vmem((n, nodes, share + 8, half), F32),
        vmem((n, 2, chips, share + 8, half), F32), vmem((n, 2, 2, half, half), F32), vmem((n, 2, 8, half), F32),
        vmem((2, columns, half), F32), vmem((n, columns, columns), F32), vmem((rows, columns), F32),
        vmem((n, columns, columns), F32),
        dma((4,)), dma((n, 2)), dma((n, 2)), dma((n, side)), dma((n, side)), dma((n, side, side)), dma((n, side, side)),
    ]
    scratch += [dma((n, side))] * 12
    scratch += [dma((n,)), dma((n,)), dma((n, 2)), dma((n, 2)), dma((n, nodes)), dma((n, nodes))]
    scratch += [dma((n, 2, chips))] * 2 + [dma((n, 2, nodes))] * 2 + [dma((n, 2))] * 2
    return pl.pallas_call(
        functools.partial(kernel, nodes, parts, 1.0 / (rows * parts)),
        out_shape=(
            jax.ShapeDtypeStruct((rows, columns), F32),
            jax.ShapeDtypeStruct((n, columns, columns), F32),
        ),
        in_specs=[anywhere, anywhere, pl.BlockSpec(memory_space=pltpu.SMEM), anywhere, anywhere],
        out_specs=(anywhere, anywhere),
        scratch_shapes=scratch,
        compiler_params=pltpu.CompilerParams(
            collective_id=0, has_side_effects=True, vmem_limit_bytes=60 * 1024 * 1024
        ),
    )(subspace, inverse[0], weights, diag_tiles, upper_tiles)


def solution(mesh):
    placed = (
        P("rows", None),
        P("node", None, "rows", None),
        P("node", None),
        P("rows", None),
        P("rows", None),
    )
    return jax.shard_map(
        per_device, mesh=mesh, in_specs=placed, out_specs=(P("rows", None), P()), check_vma=False
    )
```

```python
import functools

import jax
import jax.numpy as jnp
from jax import lax
from jax.experimental import pallas as pl
from jax.experimental.pallas import tpu as pltpu
from jax.sharding import PartitionSpec as P

ITERS = 2
MESH = pl.DeviceIdType.MESH
F32, BF16 = jnp.float32, jnp.bfloat16
precise = lax.Precision.HIGHEST


def dot(a, b, ca=1, cb=0, precision=None):
    return lax.dot_general(
        a, b, (((ca,), (cb,)), ((), ())), precision=precision, preferred_element_type=F32
    )


def split3(x):
    high = x.astype(BF16)
    rest = x - high.astype(F32)
    middle = rest.astype(BF16)
    low = (rest - middle.astype(F32)).astype(BF16)
    return high, middle, low


def panel_step(a, k, size):
    r0 = 8 * k
    half, lane0 = r0 // 128, r0 % 128
    halves = size // 128
    row = [[jnp.broadcast_to(a[h, r0 + i : r0 + i + 1, :], (8, 128)) for h in range(halves)] for i in range(8)]
    e = [
        [jnp.broadcast_to(row[i][half][:, lane0 + j : lane0 + j + 1], (8, 128)) for j in range(i + 1)]
        for i in range(8)
    ]
    t = [[None] * 8 for _ in range(8)]
    for j in range(8):
        r = lax.rsqrt(e[j][j])
        for q in range(j):
            t[j][q] = t[j][q] * r
        t[j][j] = r
        m = {i: e[i][j] * r for i in range(j + 1, 8)}
        for i in range(j + 1, 8):
            for q in range(j + 1, i + 1):
                e[i][q] = e[i][q] - m[i] * m[q]
            for q in range(j + 1):
                prev = t[i][q]
                t[i][q] = -m[i] * t[j][q] if prev is None else prev - m[i] * t[j][q]
    sub = lax.broadcasted_iota(jnp.int32, (8, 128), 0)
    lane = lax.broadcasted_iota(jnp.int32, (8, 128), 1)
    out = [jnp.zeros((8, 128), F32) for _ in range(halves)]
    diag = jnp.zeros((8, 128), F32)
    for q in range(8):
        col = jnp.zeros((8, 128), F32)
        for i in range(q, 8):
            col = jnp.where(sub == i, t[i][q], col)
        for h in range(halves):
            out[h] = out[h] + col * row[q][h]
        diag = jnp.where(lane == lane0 + q, col, diag)
    inside = (lane >= lane0) & (lane < lane0 + 8)
    new = [jnp.where(inside, diag, out[h]) if h == half else out[h] for h in range(halves)]
    for h in range(halves):
        a[h, r0 : r0 + 8, :] = new[h]
    if r0 + 8 >= size:
        return
    below = size - r0 - 8
    base = 128 * ((r0 + 8) // 128)
    lh, lm, ll = split3(jnp.concatenate([out[h] for h in range(base // 128, halves)], axis=1))
    rh, rm, rl = split3(jnp.concatenate(new, axis=1))
    left = jnp.concatenate([lh, lh, lm, lh, ll, lm], axis=0)
    right = jnp.concatenate([rh, rm, rh, rl, rh, rm], axis=0)
    update = dot(left, right, 0, 0)
    off = r0 + 8 - base
    for h in range(halves):
        old = a[h, r0 + 8 : size, :]
        if h == half:
            lanes = lax.broadcasted_iota(jnp.int32, (below, 128), 1)
            old = jnp.where((lanes >= lane0) & (lanes < lane0 + 8), 0.0, old)
        a[h, r0 + 8 : size, :] = old - update[off:, 128 * h : 128 * h + 128]


def packed(whole):
    half = whole.shape[0] // 2
    rows = lax.broadcasted_iota(jnp.int32, (half, half), 0)
    columns = lax.broadcasted_iota(jnp.int32, (half, half), 1)
    last = whole[half:, half:]
    row = jnp.sum(jnp.where(rows == columns, last, 0.0), axis=0, keepdims=True)
    return jnp.where(rows <= columns, whole[:half, :half], last), whole[:half, half:], row


def unpacked(first, second, row):
    half = first.shape[0]
    rows = lax.broadcasted_iota(jnp.int32, (half, half), 0)
    columns = lax.broadcasted_iota(jnp.int32, (half, half), 1)
    turned = first.T
    last = jnp.where(rows > columns, first, jnp.where(rows < columns, turned, row))
    return jnp.where(rows <= columns, first, turned), second, last


def kernel(
    nodes, parts, scale,
    subspace, inverse, weights, diag_in, upper_in, out, projected,
    current, blocks, diag, upper, firsts, ups, from_next, from_prior, edge,
    term, ra, rb, pa, pb, qa, qb, field, next_rows, imaged,
    block, mine, pair, pk, grs, zb, res, rest, a, inv,
    load, tip_send, tip_recv, rsa_send, rsa_recv, rsb_send, rsb_recv,
    rsc_send, rsc_recv, rsd_send, rsd_recv,
    aga_send, aga_recv, agb_send, agb_recv, agc_send, agc_recv, agd_send, agd_recv,
    row_send, row_recv, pair_send, pair_recv, grs_send, grs_recv,
    z_send, z_recv, all_send, all_recv, fin_send, fin_recv,
):
    j, p = lax.axis_index("node"), lax.axis_index("rows")
    side = int(round(nodes**0.5))
    x, y = j // side, lax.rem(j, side)
    core = lax.rem(p, 2)
    sibling = p + 1 - 2 * core
    up, down = lax.rem(p + 1, parts), lax.rem(p + parts - 1, parts)
    cross = lax.rem(p + parts - 1 + 2 * core, parts)
    chips = parts // 2
    z = p // 2
    size, columns = current.shape
    band = diag.shape[1]
    piece = size // nodes // 2
    half = columns // 2
    share = half // nodes

    def each(start, stop, act):
        for k in range(start, stop):
            act(k)

    def added(start, stop, add, total):
        for k in range(start, stop):
            total = add(k, total)
        return total

    def turn(value, k, count):
        return lax.rem(value + k, count)

    def copy(src, dst, send, recv, device):
        return pltpu.make_async_remote_copy(
            src_ref=src, dst_ref=dst, send_sem=send, recv_sem=recv, device_id=device, device_id_type=MESH
        )

    loads = [
        pltpu.make_async_copy(subspace, current, load.at[0]),
        pltpu.make_async_copy(inverse, blocks, load.at[1]),
        pltpu.make_async_copy(upper_in, upper, load.at[2]),
        pltpu.make_async_copy(diag_in, diag, load.at[3]),
    ]
    for item in loads:
        item.start()
    barrier = pltpu.get_barrier_semaphore()

    def greet(device):
        pl.semaphore_signal(barrier, inc=1, device_id=device, device_id_type=MESH)

    each(1, chips, lambda k: greet((j, turn(p, 2 * k, parts))))
    each(1, nodes, lambda k: greet((turn(j, k, nodes), p)))
    greet((j, cross))
    greet((j, sibling))
    for item in loads:
        item.wait()
    w0, w1 = weights[0, 0], weights[0, 1]

    def tips(it, ready):
        tip_down, tip_up = tip_copies(it)
        coupling = upper[size - band :, :]
        for part in range(2):
            firsts[part] = dot(blocks[part, :band, :], current[...]).astype(BF16)
        if ready:
            tip_down.start()
        for part in range(2):
            last = dot(blocks[part, size - band :, :], current[...]).astype(BF16).astype(F32)
            ups[part] = dot(coupling, last, 0, 0, precise).astype(BF16)
        if not ready:
            pl.semaphore_wait(barrier, nodes - 1 + chips - 1 + 2)
            tip_down.start()
        tip_up.start()

    def pair_copy(it, m):
        return copy(block.at[m], pair.at[it, m], pair_send.at[it, m], pair_recv.at[it, m], (j, sibling))

    def pack_start(it, m, whole):
        first, second, row = packed(whole)
        mine[m] = jnp.where(core == 0, first, second)
        block[m, :half, :] = jnp.where(core == 0, second, first)
        block[m, half:, :] = jnp.broadcast_to(row, (8, half))
        pair_copy(it, m).start()

    def pack_sum(it, m):
        pair_copy(it, m).wait()
        total = mine[m] + pair[it, m, :half, :]
        pk[m, :, :share, :] = total.reshape(nodes, share, half)
        row = block[m, half:, :] + pair[it, m, half:, :]
        pk[m, :, share:, :] = jnp.broadcast_to(row[None], (nodes, 8, half))

    slice_rows = pl.ds(0, share + 1)

    def grs_copy(it, source, to):
        return copy(
            pk.at[0, to, slice_rows, :], grs.at[it, source, slice_rows, :],
            grs_send.at[it, to], grs_recv.at[it, source], (to, p),
        )

    def z_copy(it, m, source, to):
        here = zb.at[it, m, source, slice_rows, :]
        return copy(here, here, z_send.at[it, m, to], z_recv.at[it, m, source], (j, 2 * to + core))

    def z_start(it, m, value):
        zb[it, m, z, slice_rows, :] = value
        each(1, chips, lambda k: z_copy(it, m, z, turn(z, k, chips)).start())

    def all_copy(it, m, source, to):
        here = res.at[it, m, core, pl.ds(pl.multiple_of(source * share, 8), share), :]
        return copy(here, here, all_send.at[it, m, to], all_recv.at[it, m, source], (to, p))

    def z_finish(it, m):
        def add(k, total):
            source = turn(z, chips - k, chips)
            z_copy(it, m, source, source).wait_recv()
            return total + zb[it, m, source, slice_rows, :]

        total = added(1, chips, add, zb[it, m, z, slice_rows, :])
        rest[it, m] = jnp.broadcast_to(total[share : share + 1, :], (8, half))
        res[it, m, core, pl.ds(pl.multiple_of(j * share, 8), share), :] = total[:share, :]
        each(1, nodes, lambda k: all_copy(it, m, j, turn(j, k, nodes)).start())

    def fin_copy(it, m, which):
        here = res.at[it, m, which]
        return copy(here, here, fin_send.at[it, m], fin_recv.at[it, m], (j, sibling))

    def all_finish(it, m):
        def wait(k):
            source = turn(j, nodes - k, nodes)
            all_copy(it, m, source, source).wait_recv()

        each(1, nodes, wait)
        fin_copy(it, m, core).start()

    def summed(it, m):
        fin_copy(it, m, 1 - core).wait_recv()
        return unpacked(res[it, m, 0], res[it, m, 1], rest[it, m, 0:1, :])

    def project(it):
        first, second, last = summed(it, 1)
        whole = jnp.concatenate(
            [jnp.concatenate([first, second], axis=1), jnp.concatenate([second.T, last], axis=1)], axis=0
        )
        left = dot(inv[it], whole * scale, 1, 0, precise)
        projected[it] = dot(left, inv[it], 1, 1, precise)

    def drained(it):
        row_copy(it).wait_send()

        def over_side(k):
            xx, yy = turn(x, k, side), turn(y, k, side)
            rsa_copy(it, xx, x).wait_send()
            rsc_copy(it, yy, y).wait_send()
            rsd_copy(it, xx, x).wait_send()
            aga_copy(it, xx, x).wait_send()
            agb_copy(it, yy, y).wait_send()
            agc_copy(it, yy, y).wait_send()
            agd_copy(it, xx, x).wait_send()
            each(0, side, lambda g: rsb_copy(it, g, yy, y).wait_send())

        each(1, side, over_side)

        def over_nodes(k):
            to = turn(j, k, nodes)
            grs_copy(it, j, to).wait_send()
            all_copy(it, 0, j, to).wait_send()

        each(1, nodes, over_nodes)
        each(1, chips, lambda k: z_copy(it, 0, z, turn(z, k, chips)).wait_send())
        each(1, chips, lambda k: z_copy(it, 1, z, turn(z, k, chips)).wait_send())
        fin_copy(it, 0, core).wait_send()

    def projected_drained(it):
        each(1, nodes, lambda k: all_copy(it, 1, j, turn(j, k, nodes)).wait_send())
        fin_copy(it, 1, core).wait_send()

    def tip_copies(it):
        return (
            copy(firsts, from_next.at[it], tip_send.at[it, 0], tip_recv.at[it, 0], (j, down)),
            copy(ups, from_prior.at[it], tip_send.at[it, 1], tip_recv.at[it, 1], (j, up)),
        )

    def rsa_copy(it, g, source):
        return copy(term.at[g, :, 0], ra.at[it, source], rsa_send.at[it, g], rsa_recv.at[it, source], (g * side + y, p))

    def rsb_copy(it, g, to, source):
        return copy(
            term.at[g, to, 1], rb.at[it, source, g], rsb_send.at[it, to, g], rsb_recv.at[it, source, g], (x * side + to, p)
        )

    def rsc_copy(it, to, source):
        return copy(pa.at[to], qa.at[it, source], rsc_send.at[it, to], rsc_recv.at[it, source], (x * side + to, p))

    def rsd_copy(it, to, source):
        return copy(pb.at[to], qb.at[it, source], rsd_send.at[it, to], rsd_recv.at[it, source], (to * side + y, p))

    def aga_copy(it, to, source):
        here = field.at[it, source, y, 0]
        return copy(here, here, aga_send.at[it, to], aga_recv.at[it, source], (to * side + y, p))

    def agb_copy(it, to, source):
        here = field.at[it, x, source, 1]
        return copy(here, here, agb_send.at[it, to], agb_recv.at[it, source], (x * side + to, p))

    def agc_copy(it, to, source):
        here = field.at[it, :, source, 0]
        return copy(here, here, agc_send.at[it, to], agc_recv.at[it, source], (x * side + to, p))

    def agd_copy(it, to, source):
        here = field.at[it, source, :, 1]
        return copy(here, here, agd_send.at[it, to], agd_recv.at[it, source], (to * side + y, p))

    def row_copy(it):
        return copy(edge, next_rows.at[it], row_send.at[it], row_recv.at[it], (j, down))

    tile = size // side

    def iteration(it, carry):
        @pl.when(it > 0)
        def _():
            drained(it - 1)

        for g in range(side):
            rows = pl.ds(g * tile, tile)
            value = w0 * dot(blocks[0, rows, :], current[...]) - w1 * dot(blocks[1, rows, :], current[...])
            term[g] = value.reshape(side, 2, piece, columns)

        @pl.when(it > 0)
        def _():
            all_finish(it - 1, 1)
            project(it - 1)
            projected_drained(it - 1)

        tip_down, tip_up = tip_copies(it)
        tip_down.wait()
        coupling = upper[size - band :, :]
        bottom = []
        for part in range(2):
            below = dot(coupling, from_next[it, part].astype(F32), 1, 0, precise).astype(BF16)
            bottom.append(jnp.where(p == parts - 1, 0.0, below.astype(F32)))
        tip_up.wait()
        top = [jnp.where(p == 0, 0.0, from_prior[it, part].astype(F32)) for part in range(2)]
        edges = jnp.concatenate(
            [w0 * e[0] - w1 * e[1] for e in (top, bottom)] + [-w0 * e[1] - w1 * e[0] for e in (top, bottom)], axis=0
        )
        edge_high = edges.astype(BF16)
        edge_low = (edges - edge_high.astype(F32)).astype(BF16)

        def group(t):
            g = turn(x, t + 1, side)
            rows = pl.ds(pl.multiple_of(g * tile, 8), tile)
            corner = jnp.concatenate(
                [blocks[part, rows, at] for part in range(2) for at in (slice(0, band), slice(size - band, size))], axis=1
            )
            change = dot(corner, edge_high) + dot(corner, edge_low)
            term[g] = term[g] + change.reshape(side, 2, piece, columns)

            @pl.when(g != x)
            def _():
                rsa_copy(it, g, x).start()

            each(1, side, lambda k: rsb_copy(it, g, turn(y, k, side), y).start())

        each(0, side, group)

        def add_a(k, total):
            source = turn(x, side - k, side)
            rsa_copy(it, source, source).wait_recv()
            return total + ra[it, source]

        pa[...] = added(1, side, add_a, term[x, :, 0])
        each(1, side, lambda k: rsc_copy(it, turn(y, k, side), y).start())

        def add_b(k, total):
            source = turn(y, side - k, side)
            each(0, side, lambda g: rsb_copy(it, g, source, source).wait_recv())
            return total + rb[it, source]

        pb[...] = added(1, side, add_b, term[:, y, 1])
        each(1, side, lambda k: rsd_copy(it, turn(x, k, side), x).start())

        def add_c(k, total):
            source = turn(y, side - k, side)
            rsc_copy(it, source, source).wait_recv()
            return total + qa[it, source]

        field[it, x, y, 0] = added(1, side, add_c, pa[y])

        def add_d(k, total):
            source = turn(x, side - k, side)
            rsd_copy(it, source, source).wait_recv()
            return total + qb[it, source]

        field[it, x, y, 1] = added(1, side, add_d, pb[x])

        own = field[it, x, y].reshape(2 * piece, columns)
        pack_start(it, 0, dot(own, own, 0, 0, precise))
        pack_sum(it, 0)
        each(1, nodes, lambda k: grs_copy(it, j, turn(j, k, nodes)).start())

        def add_g(k, total):
            source = turn(j, nodes - k, nodes)
            grs_copy(it, source, source).wait_recv()
            return total + grs[it, source, slice_rows, :]

        z_start(it, 0, added(1, nodes, add_g, pk[0, j, slice_rows, :]))

        def ag_first(k):
            aga_copy(it, turn(x, k, side), x).start()
            agb_copy(it, turn(y, k, side), y).start()

        each(1, side, ag_first)

        def ag_first_wait(k):
            aga_copy(it, turn(x, k, side), turn(x, k, side)).wait_recv()

        each(1, side, ag_first_wait)
        each(1, side, lambda k: agc_copy(it, turn(y, k, side), y).start())

        def ag_second_wait(k):
            agb_copy(it, turn(y, k, side), turn(y, k, side)).wait_recv()

        each(1, side, ag_second_wait)
        each(1, side, lambda k: agd_copy(it, turn(x, k, side), x).start())
        z_finish(it, 0)

        def ag_last_wait(k):
            agc_copy(it, turn(y, k, side), turn(y, k, side)).wait_recv()
            agd_copy(it, turn(x, k, side), turn(x, k, side)).wait_recv()

        each(1, side, ag_last_wait)
        whole = field[it].reshape(size, columns)
        edge[...] = whole[:band, :]
        row_copy(it).start()
        tiles = size // band
        for t in range(tiles - 1):
            rows = slice(t * band, t * band + band)
            imaged[rows, :] = dot(0.5 * diag[rows, :], whole[rows, :], 1, 0, precise) + dot(
                upper[rows, :], whole[t * band + band : t * band + 2 * band, :], 1, 0, precise
            )
        rows = slice(size - band, size)
        near = dot(0.5 * diag[rows, :], whole[rows, :], 1, 0, precise)
        row_copy(it).wait_recv()
        after = jnp.where(p == parts - 1, 0.0, next_rows[it])
        imaged[rows, :] = near + dot(upper[rows, :], after, 1, 0, precise)
        product = dot(whole, imaged[...], 0, 0, precise)
        pack_start(it, 1, product + product.T)

        all_finish(it, 0)
        pack_sum(it, 1)
        z_start(it, 1, pk[1, j, slice_rows, :])
        first, second, last = summed(it, 0)
        a[0, :half, :] = first * scale
        a[1, :half, :] = second * scale
        a[0, half:, :] = jnp.zeros((half, half), F32)
        a[1, half:, :] = last * scale
        steps = columns // 8
        for k in range(steps):
            if k == (3 * steps) // 4 - 1:
                z_finish(it, 1)
            panel_step(a, k, columns)
        rows = lax.broadcasted_iota(jnp.int32, (columns, columns), 0)
        cols = lax.broadcasted_iota(jnp.int32, (columns, columns), 1)
        factor = jnp.where(rows >= cols, jnp.concatenate([a[0], a[1]], axis=1), 0.0)
        inv[it] = factor
        for g in range(side):
            rows = pl.ds(g * tile, tile)
            value = dot(field[it, g].reshape(tile, columns), factor, 1, 1, precise)
            out[rows, :] = value
            current[rows, :] = value.astype(BF16)

        @pl.when(it < ITERS - 1)
        def _():
            tips(it + 1, True)

        return carry

    tips(0, False)
    lax.fori_loop(0, ITERS, iteration, 0)
    all_finish(ITERS - 1, 1)
    project(ITERS - 1)
    projected_drained(ITERS - 1)
    drained(ITERS - 1)


def per_device(subspace, inverse, weights, diag_tiles, upper_tiles):
    nodes, parts = lax.axis_size("node"), lax.axis_size("rows")
    rows, columns = subspace.shape
    band = diag_tiles.shape[1]
    side = int(round(nodes**0.5))
    piece = rows // nodes // 2
    half = columns // 2
    share = half // nodes
    chips = parts // 2
    n = ITERS
    vmem, dma = pltpu.VMEM, pltpu.SemaphoreType.DMA
    anywhere = pl.BlockSpec(memory_space=pl.ANY)
    tip = (2, band, columns)
    scratch = [
        vmem((rows, columns), BF16), vmem((2, rows, rows), BF16), vmem((rows, band), F32), vmem((rows, band), F32),
        vmem(tip, BF16), vmem(tip, BF16), vmem((n, *tip), BF16), vmem((n, *tip), BF16), vmem((band, columns), F32),
        vmem((side, side, 2, piece, columns), F32),
        vmem((n, side, side, piece, columns), F32), vmem((n, side, side, piece, columns), F32),
        vmem((side, piece, columns), F32), vmem((side, piece, columns), F32),
        vmem((n, side, piece, columns), F32), vmem((n, side, piece, columns), F32),
        vmem((n, side, side, 2, piece, columns), F32), vmem((n, band, columns), F32), vmem((rows, columns), F32),
        vmem((2, half + 8, half), F32), vmem((2, half, half), F32), vmem((n, 2, half + 8, half), F32),
        vmem((2, nodes, share + 8, half), F32), vmem((n, nodes, share + 8, half), F32),
        vmem((n, 2, chips, share + 8, half), F32), vmem((n, 2, 2, half, half), F32), vmem((n, 2, 8, half), F32),
        vmem((2, columns, half), F32), vmem((n, columns, columns), F32),
        dma((4,)), dma((n, 2)), dma((n, 2)), dma((n, side)), dma((n, side)), dma((n, side, side)), dma((n, side, side)),
    ]
    scratch += [dma((n, side))] * 12
    scratch += [dma((n,)), dma((n,)), dma((n, 2)), dma((n, 2)), dma((n, nodes)), dma((n, nodes))]
    scratch += [dma((n, 2, chips))] * 2 + [dma((n, 2, nodes))] * 2 + [dma((n, 2))] * 2
    return pl.pallas_call(
        functools.partial(kernel, nodes, parts, 1.0 / (rows * parts)),
        out_shape=(
            jax.ShapeDtypeStruct((rows, columns), F32),
            jax.ShapeDtypeStruct((n, columns, columns), F32),
        ),
        in_specs=[anywhere, anywhere, pl.BlockSpec(memory_space=pltpu.SMEM), anywhere, anywhere],
        out_specs=(pl.BlockSpec(memory_space=pltpu.VMEM),) * 2,
        scratch_shapes=scratch,
        compiler_params=pltpu.CompilerParams(
            collective_id=0, has_side_effects=True, vmem_limit_bytes=63 * 1024 * 1024
        ),
    )(subspace, inverse[0], weights, diag_tiles, upper_tiles)


def solution(mesh):
    placed = (
        P("rows", None),
        P("node", None, "rows", None),
        P("node", None),
        P("rows", None),
        P("rows", None),
    )
    return jax.shard_map(
        per_device, mesh=mesh, in_specs=placed, out_specs=(P("rows", None), P()), check_vma=False
    )
```

```python
import functools

import jax
import jax.numpy as jnp
from jax import lax
from jax.experimental import pallas as pl
from jax.experimental.pallas import tpu as pltpu
from jax.sharding import PartitionSpec as P

ITERS = 2
MESH = pl.DeviceIdType.MESH
F32, BF16 = jnp.float32, jnp.bfloat16
precise = lax.Precision.HIGHEST


def dot(a, b, ca=1, cb=0, precision=None):
    return lax.dot_general(
        a, b, (((ca,), (cb,)), ((), ())), precision=precision, preferred_element_type=F32
    )


def split3(x):
    high = x.astype(BF16)
    rest = x - high.astype(F32)
    middle = rest.astype(BF16)
    low = (rest - middle.astype(F32)).astype(BF16)
    return high, middle, low


def panel_step(a, k, size):
    r0 = 8 * k
    half, lane0 = r0 // 128, r0 % 128
    halves = size // 128
    row = [[jnp.broadcast_to(a[h, r0 + i : r0 + i + 1, :], (8, 128)) for h in range(halves)] for i in range(8)]
    e = [
        [jnp.broadcast_to(row[i][half][:, lane0 + j : lane0 + j + 1], (8, 128)) for j in range(i + 1)]
        for i in range(8)
    ]
    t = [[None] * 8 for _ in range(8)]
    for j in range(8):
        r = lax.rsqrt(e[j][j])
        for q in range(j):
            t[j][q] = t[j][q] * r
        t[j][j] = r
        m = {i: e[i][j] * r for i in range(j + 1, 8)}
        for i in range(j + 1, 8):
            for q in range(j + 1, i + 1):
                e[i][q] = e[i][q] - m[i] * m[q]
            for q in range(j + 1):
                prev = t[i][q]
                t[i][q] = -m[i] * t[j][q] if prev is None else prev - m[i] * t[j][q]
    sub = lax.broadcasted_iota(jnp.int32, (8, 128), 0)
    lane = lax.broadcasted_iota(jnp.int32, (8, 128), 1)
    out = [jnp.zeros((8, 128), F32) for _ in range(halves)]
    diag = jnp.zeros((8, 128), F32)
    for q in range(8):
        col = jnp.zeros((8, 128), F32)
        for i in range(q, 8):
            col = jnp.where(sub == i, t[i][q], col)
        for h in range(halves):
            out[h] = out[h] + col * row[q][h]
        diag = jnp.where(lane == lane0 + q, col, diag)
    inside = (lane >= lane0) & (lane < lane0 + 8)
    new = [jnp.where(inside, diag, out[h]) if h == half else out[h] for h in range(halves)]
    for h in range(halves):
        a[h, r0 : r0 + 8, :] = new[h]
    if r0 + 8 >= size:
        return
    below = size - r0 - 8
    base = 128 * ((r0 + 8) // 128)
    lh, lm, ll = split3(jnp.concatenate([out[h] for h in range(base // 128, halves)], axis=1))
    rh, rm, rl = split3(jnp.concatenate(new, axis=1))
    left = jnp.concatenate([lh, lh, lm, lh, ll, lm], axis=0)
    right = jnp.concatenate([rh, rm, rh, rl, rh, rm], axis=0)
    update = dot(left, right, 0, 0)
    off = r0 + 8 - base
    for h in range(halves):
        old = a[h, r0 + 8 : size, :]
        if h == half:
            lanes = lax.broadcasted_iota(jnp.int32, (below, 128), 1)
            old = jnp.where((lanes >= lane0) & (lanes < lane0 + 8), 0.0, old)
        a[h, r0 + 8 : size, :] = old - update[off:, 128 * h : 128 * h + 128]


def packed(whole):
    half = whole.shape[0] // 2
    rows = lax.broadcasted_iota(jnp.int32, (half, half), 0)
    columns = lax.broadcasted_iota(jnp.int32, (half, half), 1)
    last = whole[half:, half:]
    row = jnp.sum(jnp.where(rows == columns, last, 0.0), axis=0, keepdims=True)
    return jnp.where(rows <= columns, whole[:half, :half], last), whole[:half, half:], row


def unpacked(first, second, row):
    half = first.shape[0]
    rows = lax.broadcasted_iota(jnp.int32, (half, half), 0)
    columns = lax.broadcasted_iota(jnp.int32, (half, half), 1)
    turned = first.T
    last = jnp.where(rows > columns, first, jnp.where(rows < columns, turned, row))
    return jnp.where(rows <= columns, first, turned), second, last


def kernel(
    nodes, parts, scale,
    subspace, inverse, weights, diag_in, upper_in, out, projected,
    current, blocks, diag, upper, firsts, ups, from_next, from_prior, edge,
    term, ra, rb, pa, pb, qa, qb, field, next_rows, imaged,
    block, mine, pair, pk, grs, zb, res, rest, a, inv,
    load, tip_send, tip_recv, rsa_send, rsa_recv, rsb_send, rsb_recv,
    rsc_send, rsc_recv, rsd_send, rsd_recv,
    aga_send, aga_recv, agb_send, agb_recv, agc_send, agc_recv, agd_send, agd_recv,
    row_send, row_recv, pair_send, pair_recv, grs_send, grs_recv,
    z_send, z_recv, all_send, all_recv, fin_send, fin_recv,
):
    j, p = lax.axis_index("node"), lax.axis_index("rows")
    side = int(round(nodes**0.5))
    x, y = j // side, lax.rem(j, side)
    core = lax.rem(p, 2)
    sibling = p + 1 - 2 * core
    up, down = lax.rem(p + 1, parts), lax.rem(p + parts - 1, parts)
    cross = lax.rem(p + parts - 1 + 2 * core, parts)
    chips = parts // 2
    z = p // 2
    size, columns = current.shape
    band = diag.shape[1]
    piece = size // nodes // 2
    half = columns // 2
    share = half // nodes

    def each(start, stop, act):
        for k in range(start, stop):
            act(k)

    def added(start, stop, add, total):
        for k in range(start, stop):
            total = add(k, total)
        return total

    def turn(value, k, count):
        return lax.rem(value + k, count)

    def copy(src, dst, send, recv, device):
        return pltpu.make_async_remote_copy(
            src_ref=src, dst_ref=dst, send_sem=send, recv_sem=recv, device_id=device, device_id_type=MESH
        )

    loads = [
        pltpu.make_async_copy(subspace, current, load.at[0]),
        pltpu.make_async_copy(inverse, blocks, load.at[1]),
        pltpu.make_async_copy(upper_in, upper, load.at[2]),
        pltpu.make_async_copy(diag_in, diag, load.at[3]),
    ]
    for item in loads:
        item.start()
    barrier = pltpu.get_barrier_semaphore()

    def greet(device):
        pl.semaphore_signal(barrier, inc=1, device_id=device, device_id_type=MESH)

    each(1, chips, lambda k: greet((j, turn(p, 2 * k, parts))))
    each(1, nodes, lambda k: greet((turn(j, k, nodes), p)))
    greet((j, cross))
    greet((j, sibling))
    for item in loads:
        item.wait()
    w0, w1 = weights[0, 0], weights[0, 1]

    def tips(it, ready):
        tip_down, tip_up = tip_copies(it)
        coupling = upper[size - band :, :]
        for part in range(2):
            firsts[part] = dot(blocks[part, :band, :], current[...]).astype(BF16)
        if ready:
            tip_down.start()
        for part in range(2):
            last = dot(blocks[part, size - band :, :], current[...]).astype(BF16).astype(F32)
            ups[part] = dot(coupling, last, 0, 0, precise).astype(BF16)
        if not ready:
            pl.semaphore_wait(barrier, nodes - 1 + chips - 1 + 2)
            tip_down.start()
        tip_up.start()

    def pair_copy(it, m):
        return copy(block.at[m], pair.at[it, m], pair_send.at[it, m], pair_recv.at[it, m], (j, sibling))

    def pack_start(it, m, whole):
        first, second, row = packed(whole)
        mine[m] = jnp.where(core == 0, first, second)
        block[m, :half, :] = jnp.where(core == 0, second, first)
        block[m, half:, :] = jnp.broadcast_to(row, (8, half))
        pair_copy(it, m).start()

    def pack_sum(it, m):
        pair_copy(it, m).wait()
        total = mine[m] + pair[it, m, :half, :]
        pk[m, :, :share, :] = total.reshape(nodes, share, half)
        row = block[m, half:, :] + pair[it, m, half:, :]
        pk[m, :, share:, :] = jnp.broadcast_to(row[None], (nodes, 8, half))

    slice_rows = pl.ds(0, share + 1)

    def grs_copy(it, source, to):
        return copy(
            pk.at[0, to, slice_rows, :], grs.at[it, source, slice_rows, :],
            grs_send.at[it, to], grs_recv.at[it, source], (to, p),
        )

    def z_copy(it, m, source, to):
        here = zb.at[it, m, source, slice_rows, :]
        return copy(here, here, z_send.at[it, m, to], z_recv.at[it, m, source], (j, 2 * to + core))

    def z_start(it, m, value):
        zb[it, m, z, slice_rows, :] = value
        each(1, chips, lambda k: z_copy(it, m, z, turn(z, k, chips)).start())

    def all_copy(it, m, source, to):
        here = res.at[it, m, core, pl.ds(pl.multiple_of(source * share, 8), share), :]
        return copy(here, here, all_send.at[it, m, to], all_recv.at[it, m, source], (to, p))

    def z_finish(it, m):
        def add(k, total):
            source = turn(z, chips - k, chips)
            z_copy(it, m, source, source).wait_recv()
            return total + zb[it, m, source, slice_rows, :]

        total = added(1, chips, add, zb[it, m, z, slice_rows, :])
        rest[it, m] = jnp.broadcast_to(total[share : share + 1, :], (8, half))
        res[it, m, core, pl.ds(pl.multiple_of(j * share, 8), share), :] = total[:share, :]
        each(1, nodes, lambda k: all_copy(it, m, j, turn(j, k, nodes)).start())

    def fin_copy(it, m, which):
        here = res.at[it, m, which]
        return copy(here, here, fin_send.at[it, m], fin_recv.at[it, m], (j, sibling))

    def all_finish(it, m):
        def wait(k):
            source = turn(j, nodes - k, nodes)
            all_copy(it, m, source, source).wait_recv()

        each(1, nodes, wait)
        fin_copy(it, m, core).start()

    def summed(it, m):
        fin_copy(it, m, 1 - core).wait_recv()
        return unpacked(res[it, m, 0], res[it, m, 1], rest[it, m, 0:1, :])

    def project(it):
        first, second, last = summed(it, 1)
        whole = jnp.concatenate(
            [jnp.concatenate([first, second], axis=1), jnp.concatenate([second.T, last], axis=1)], axis=0
        )
        left = dot(inv[it], whole * scale, 1, 0, precise)
        projected[it] = dot(left, inv[it], 1, 1, precise)

    def drained(it):
        row_copy(it).wait_send()

        def over_side(k):
            xx, yy = turn(x, k, side), turn(y, k, side)
            rsa_copy(it, xx, x).wait_send()
            rsc_copy(it, yy, y).wait_send()
            rsd_copy(it, xx, x).wait_send()
            aga_copy(it, xx, x).wait_send()
            agb_copy(it, yy, y).wait_send()
            agc_copy(it, yy, y).wait_send()
            agd_copy(it, xx, x).wait_send()
            each(0, side, lambda g: rsb_copy(it, g, yy, y).wait_send())

        each(1, side, over_side)

        def over_nodes(k):
            to = turn(j, k, nodes)
            grs_copy(it, j, to).wait_send()
            all_copy(it, 0, j, to).wait_send()

        each(1, nodes, over_nodes)
        each(1, chips, lambda k: z_copy(it, 0, z, turn(z, k, chips)).wait_send())
        each(1, chips, lambda k: z_copy(it, 1, z, turn(z, k, chips)).wait_send())
        fin_copy(it, 0, core).wait_send()

    def projected_drained(it):
        each(1, nodes, lambda k: all_copy(it, 1, j, turn(j, k, nodes)).wait_send())
        fin_copy(it, 1, core).wait_send()

    def tip_copies(it):
        return (
            copy(firsts, from_next.at[it], tip_send.at[it, 0], tip_recv.at[it, 0], (j, down)),
            copy(ups, from_prior.at[it], tip_send.at[it, 1], tip_recv.at[it, 1], (j, up)),
        )

    def rsa_copy(it, g, source):
        return copy(term.at[g, :, 0], ra.at[it, source], rsa_send.at[it, g], rsa_recv.at[it, source], (g * side + y, p))

    def rsb_copy(it, g, to, source):
        return copy(
            term.at[g, to, 1], rb.at[it, source, g], rsb_send.at[it, to, g], rsb_recv.at[it, source, g], (x * side + to, p)
        )

    def rsc_copy(it, to, source):
        return copy(pa.at[to], qa.at[it, source], rsc_send.at[it, to], rsc_recv.at[it, source], (x * side + to, p))

    def rsd_copy(it, to, source):
        return copy(pb.at[to], qb.at[it, source], rsd_send.at[it, to], rsd_recv.at[it, source], (to * side + y, p))

    def aga_copy(it, to, source):
        here = field.at[it, source, y, 0]
        return copy(here, here, aga_send.at[it, to], aga_recv.at[it, source], (to * side + y, p))

    def agb_copy(it, to, source):
        here = field.at[it, x, source, 1]
        return copy(here, here, agb_send.at[it, to], agb_recv.at[it, source], (x * side + to, p))

    def agc_copy(it, to, source):
        here = field.at[it, :, source, 0]
        return copy(here, here, agc_send.at[it, to], agc_recv.at[it, source], (x * side + to, p))

    def agd_copy(it, to, source):
        here = field.at[it, source, :, 1]
        return copy(here, here, agd_send.at[it, to], agd_recv.at[it, source], (to * side + y, p))

    def row_copy(it):
        return copy(edge, next_rows.at[it], row_send.at[it], row_recv.at[it], (j, down))

    tile = size // side

    def iteration(it, carry):
        @pl.when(it > 0)
        def _():
            drained(it - 1)

        for g in range(side):
            rows = pl.ds(g * tile, tile)
            value = w0 * dot(blocks[0, rows, :], current[...]) - w1 * dot(blocks[1, rows, :], current[...])
            term[g] = value.reshape(side, 2, piece, columns)

        @pl.when(it > 0)
        def _():
            all_finish(it - 1, 1)
            project(it - 1)
            projected_drained(it - 1)

        tip_down, tip_up = tip_copies(it)
        tip_down.wait()
        coupling = upper[size - band :, :]
        bottom = []
        for part in range(2):
            below = dot(coupling, from_next[it, part].astype(F32), 1, 0, precise).astype(BF16)
            bottom.append(jnp.where(p == parts - 1, 0.0, below.astype(F32)))
        tip_up.wait()
        top = [jnp.where(p == 0, 0.0, from_prior[it, part].astype(F32)) for part in range(2)]
        edges = jnp.concatenate(
            [w0 * e[0] - w1 * e[1] for e in (top, bottom)] + [-w0 * e[1] - w1 * e[0] for e in (top, bottom)], axis=0
        )
        edge_high = edges.astype(BF16)
        edge_low = (edges - edge_high.astype(F32)).astype(BF16)

        def group(t):
            g = turn(x, t + 1, side)
            rows = pl.ds(pl.multiple_of(g * tile, 8), tile)
            corner = jnp.concatenate(
                [blocks[part, rows, at] for part in range(2) for at in (slice(0, band), slice(size - band, size))], axis=1
            )
            change = dot(corner, edge_high) + dot(corner, edge_low)
            term[g] = term[g] + change.reshape(side, 2, piece, columns)

            @pl.when(g != x)
            def _():
                rsa_copy(it, g, x).start()

            each(1, side, lambda k: rsb_copy(it, g, turn(y, k, side), y).start())

        each(0, side, group)

        def add_a(k, total):
            source = turn(x, side - k, side)
            rsa_copy(it, source, source).wait_recv()
            return total + ra[it, source]

        pa[...] = added(1, side, add_a, term[x, :, 0])
        each(1, side, lambda k: rsc_copy(it, turn(y, k, side), y).start())

        def add_b(k, total):
            source = turn(y, side - k, side)
            each(0, side, lambda g: rsb_copy(it, g, source, source).wait_recv())
            return total + rb[it, source]

        pb[...] = added(1, side, add_b, term[:, y, 1])
        each(1, side, lambda k: rsd_copy(it, turn(x, k, side), x).start())

        def add_c(k, total):
            source = turn(y, side - k, side)
            rsc_copy(it, source, source).wait_recv()
            return total + qa[it, source]

        field[it, x, y, 0] = added(1, side, add_c, pa[y])

        def add_d(k, total):
            source = turn(x, side - k, side)
            rsd_copy(it, source, source).wait_recv()
            return total + qb[it, source]

        field[it, x, y, 1] = added(1, side, add_d, pb[x])

        own = field[it, x, y].reshape(2 * piece, columns)
        pack_start(it, 0, dot(own, own, 0, 0, precise))
        pack_sum(it, 0)
        each(1, nodes, lambda k: grs_copy(it, j, turn(j, k, nodes)).start())

        def add_g(k, total):
            source = turn(j, nodes - k, nodes)
            grs_copy(it, source, source).wait_recv()
            return total + grs[it, source, slice_rows, :]

        z_start(it, 0, added(1, nodes, add_g, pk[0, j, slice_rows, :]))

        def ag_first(k):
            aga_copy(it, turn(x, k, side), x).start()
            agb_copy(it, turn(y, k, side), y).start()

        each(1, side, ag_first)

        def ag_first_wait(k):
            aga_copy(it, turn(x, k, side), turn(x, k, side)).wait_recv()

        each(1, side, ag_first_wait)
        each(1, side, lambda k: agc_copy(it, turn(y, k, side), y).start())

        def ag_second_wait(k):
            agb_copy(it, turn(y, k, side), turn(y, k, side)).wait_recv()

        each(1, side, ag_second_wait)
        each(1, side, lambda k: agd_copy(it, turn(x, k, side), x).start())
        z_finish(it, 0)

        def ag_last_wait(k):
            agc_copy(it, turn(y, k, side), turn(y, k, side)).wait_recv()
            agd_copy(it, turn(x, k, side), turn(x, k, side)).wait_recv()

        each(1, side, ag_last_wait)
        whole = field[it].reshape(size, columns)
        edge[...] = whole[:band, :]
        row_copy(it).start()
        tiles = size // band
        for t in range(tiles - 1):
            rows = slice(t * band, t * band + band)
            imaged[rows, :] = dot(0.5 * diag[rows, :], whole[rows, :], 1, 0, precise) + dot(
                upper[rows, :], whole[t * band + band : t * band + 2 * band, :], 1, 0, precise
            )
        all_finish(it, 0)
        rows = slice(size - band, size)
        near = dot(0.5 * diag[rows, :], whole[rows, :], 1, 0, precise)
        row_copy(it).wait_recv()
        after = jnp.where(p == parts - 1, 0.0, next_rows[it])
        imaged[rows, :] = near + dot(upper[rows, :], after, 1, 0, precise)
        product = dot(whole, imaged[...], 0, 0, precise)
        pack_start(it, 1, product + product.T)
        first, second, last = summed(it, 0)
        a[0, :half, :] = first * scale
        a[1, :half, :] = second * scale
        a[0, half:, :] = jnp.zeros((half, half), F32)
        a[1, half:, :] = last * scale
        steps = columns // 8
        for k in range(steps):
            if k == steps // 8 - 1:
                pack_sum(it, 1)
                z_start(it, 1, pk[1, j, slice_rows, :])
            if k == (13 * steps) // 16:
                z_finish(it, 1)
            panel_step(a, k, columns)
        rows = lax.broadcasted_iota(jnp.int32, (columns, columns), 0)
        cols = lax.broadcasted_iota(jnp.int32, (columns, columns), 1)
        factor = jnp.where(rows >= cols, jnp.concatenate([a[0], a[1]], axis=1), 0.0)
        inv[it] = factor
        for g in range(side):
            rows = pl.ds(g * tile, tile)
            value = dot(field[it, g].reshape(tile, columns), factor, 1, 1, precise)
            out[rows, :] = value
            current[rows, :] = value.astype(BF16)

        @pl.when(it < ITERS - 1)
        def _():
            tips(it + 1, True)

        return carry

    tips(0, False)
    lax.fori_loop(0, ITERS, iteration, 0)
    all_finish(ITERS - 1, 1)
    project(ITERS - 1)
    projected_drained(ITERS - 1)
    drained(ITERS - 1)


def finish_kernel(ortho, projected, ortho_out, projected_out, ortho_held, projected_held, come, go):
    count = come.shape[0] // 2
    rows = ortho.shape[0] // count
    wide = projected.shape[1] // count
    places = []
    for k in range(count):
        at = pl.ds(k * rows, rows)
        places.append((ortho.at[at], ortho_held.at[at], ortho_out.at[at]))
    for k in range(count):
        at = pl.ds(k * wide, wide)
        places.append((projected.at[:, at], projected_held.at[:, at], projected_out.at[:, at]))
    into = [pltpu.make_async_copy(a, b, come.at[k]) for k, (a, b, _) in enumerate(places)]
    onward = [pltpu.make_async_copy(b, c, go.at[k]) for k, (_, b, c) in enumerate(places)]
    for item in into:
        item.start()
    for first, second in zip(into, onward):
        first.wait()
        second.start()
    for item in onward:
        item.wait()


def finished(ortho, projected):
    anywhere = pl.BlockSpec(memory_space=pl.ANY)
    return pl.pallas_call(
        finish_kernel,
        out_shape=tuple(jax.ShapeDtypeStruct(v.shape, v.dtype) for v in (ortho, projected)),
        in_specs=[anywhere] * 2,
        out_specs=(anywhere,) * 2,
        scratch_shapes=[pltpu.VMEM(v.shape, v.dtype) for v in (ortho, projected)]
        + [pltpu.SemaphoreType.DMA((8,))] * 2,
        compiler_params=pltpu.CompilerParams(vmem_limit_bytes=62 * 1024 * 1024),
    )(ortho, projected)


def per_device(subspace, inverse, weights, diag_tiles, upper_tiles):
    nodes, parts = lax.axis_size("node"), lax.axis_size("rows")
    rows, columns = subspace.shape
    band = diag_tiles.shape[1]
    side = int(round(nodes**0.5))
    piece = rows // nodes // 2
    half = columns // 2
    share = half // nodes
    chips = parts // 2
    n = ITERS
    vmem, dma = pltpu.VMEM, pltpu.SemaphoreType.DMA
    anywhere = pl.BlockSpec(memory_space=pl.ANY)
    tip = (2, band, columns)
    scratch = [
        vmem((rows, columns), BF16), vmem((2, rows, rows), BF16), vmem((rows, band), F32), vmem((rows, band), F32),
        vmem(tip, BF16), vmem(tip, BF16), vmem((n, *tip), BF16), vmem((n, *tip), BF16), vmem((band, columns), F32),
        vmem((side, side, 2, piece, columns), F32),
        vmem((n, side, side, piece, columns), F32), vmem((n, side, side, piece, columns), F32),
        vmem((side, piece, columns), F32), vmem((side, piece, columns), F32),
        vmem((n, side, piece, columns), F32), vmem((n, side, piece, columns), F32),
        vmem((n, side, side, 2, piece, columns), F32), vmem((n, band, columns), F32), vmem((rows, columns), F32),
        vmem((2, half + 8, half), F32), vmem((2, half, half), F32), vmem((n, 2, half + 8, half), F32),
        vmem((2, nodes, share + 8, half), F32), vmem((n, nodes, share + 8, half), F32),
        vmem((n, 2, chips, share + 8, half), F32), vmem((n, 2, 2, half, half), F32), vmem((n, 2, 8, half), F32),
        vmem((2, columns, half), F32), vmem((n, columns, columns), F32),
        dma((4,)), dma((n, 2)), dma((n, 2)), dma((n, side)), dma((n, side)), dma((n, side, side)), dma((n, side, side)),
    ]
    scratch += [dma((n, side))] * 12
    scratch += [dma((n,)), dma((n,)), dma((n, 2)), dma((n, 2)), dma((n, nodes)), dma((n, nodes))]
    scratch += [dma((n, 2, chips))] * 2 + [dma((n, 2, nodes))] * 2 + [dma((n, 2))] * 2
    results = pl.pallas_call(
        functools.partial(kernel, nodes, parts, 1.0 / (rows * parts)),
        out_shape=(
            jax.ShapeDtypeStruct((rows, columns), F32),
            jax.ShapeDtypeStruct((n, columns, columns), F32),
        ),
        in_specs=[anywhere, anywhere, pl.BlockSpec(memory_space=pltpu.SMEM), anywhere, anywhere],
        out_specs=(pl.BlockSpec(memory_space=pltpu.VMEM),) * 2,
        scratch_shapes=scratch,
        compiler_params=pltpu.CompilerParams(
            collective_id=0, has_side_effects=True, vmem_limit_bytes=62 * 1024 * 1024
        ),
    )(subspace, inverse[0], weights, diag_tiles, upper_tiles)
    return finished(*results)


def solution(mesh):
    placed = (
        P("rows", None),
        P("node", None, "rows", None),
        P("node", None),
        P("rows", None),
        P("rows", None),
    )
    return jax.shard_map(
        per_device, mesh=mesh, in_specs=placed, out_specs=(P("rows", None), P()), check_vma=False
    )
```

```python
import functools

import jax
import jax.numpy as jnp
from jax import lax
from jax.experimental import pallas as pl
from jax.experimental.pallas import tpu as pltpu
from jax.sharding import PartitionSpec as P

ITERS = 2
MESH = pl.DeviceIdType.MESH
F32, BF16 = jnp.float32, jnp.bfloat16
precise = lax.Precision.HIGHEST


def dot(a, b, ca=1, cb=0, precision=None):
    return lax.dot_general(
        a, b, (((ca,), (cb,)), ((), ())), precision=precision, preferred_element_type=F32
    )


def split3(x):
    high = x.astype(BF16)
    rest = x - high.astype(F32)
    middle = rest.astype(BF16)
    low = (rest - middle.astype(F32)).astype(BF16)
    return high, middle, low


def panel_step(a, k, size):
    r0 = 8 * k
    half, lane0 = r0 // 128, r0 % 128
    halves = size // 128
    row = [[a[h, pl.ds(r0 + i, 8, stride=0), :] for h in range(halves)] for i in range(8)]
    e = [
        [jnp.broadcast_to(row[i][half][:, lane0 + j : lane0 + j + 1], (8, 128)) for j in range(i + 1)]
        for i in range(8)
    ]
    t = [[None] * 8 for _ in range(8)]
    for j in range(8):
        r = lax.rsqrt(e[j][j])
        for q in range(j):
            t[j][q] = t[j][q] * r
        t[j][j] = r
        m = {i: e[i][j] * r for i in range(j + 1, 8)}
        for i in range(j + 1, 8):
            for q in range(j + 1, i + 1):
                e[i][q] = e[i][q] - m[i] * m[q]
            for q in range(j + 1):
                prev = t[i][q]
                t[i][q] = -m[i] * t[j][q] if prev is None else prev - m[i] * t[j][q]
    sub = lax.broadcasted_iota(jnp.int32, (8, 128), 0)
    lane = lax.broadcasted_iota(jnp.int32, (8, 128), 1)
    out = [jnp.zeros((8, 128), F32) for _ in range(halves)]
    diag = jnp.zeros((8, 128), F32)
    for q in range(8):
        col = jnp.zeros((8, 128), F32)
        for i in range(q, 8):
            col = jnp.where(sub == i, t[i][q], col)
        for h in range(halves):
            out[h] = out[h] + col * row[q][h]
        diag = jnp.where(lane == lane0 + q, col, diag)
    inside = (lane >= lane0) & (lane < lane0 + 8)
    new = [jnp.where(inside, diag, out[h]) if h == half else out[h] for h in range(halves)]
    for h in range(halves):
        a[h, r0 : r0 + 8, :] = new[h]
    if r0 + 8 >= size:
        return
    below = size - r0 - 8
    base = 128 * ((r0 + 8) // 128)
    lh, lm, ll = split3(jnp.concatenate([out[h] for h in range(base // 128, halves)], axis=1))
    rh, rm, rl = split3(jnp.concatenate(new, axis=1))
    left = jnp.concatenate([lh, lh, lm, lh, ll, lm], axis=0)
    right = jnp.concatenate([rh, rm, rh, rl, rh, rm], axis=0)
    update = dot(left, right, 0, 0)
    off = r0 + 8 - base
    for h in range(halves):
        old = a[h, r0 + 8 : size, :]
        if h == half:
            lanes = lax.broadcasted_iota(jnp.int32, (below, 128), 1)
            old = jnp.where((lanes >= lane0) & (lanes < lane0 + 8), 0.0, old)
        a[h, r0 + 8 : size, :] = old - update[off:, 128 * h : 128 * h + 128]


def packed(whole):
    half = whole.shape[0] // 2
    rows = lax.broadcasted_iota(jnp.int32, (half, half), 0)
    columns = lax.broadcasted_iota(jnp.int32, (half, half), 1)
    last = whole[half:, half:]
    row = jnp.sum(jnp.where(rows == columns, last, 0.0), axis=0, keepdims=True)
    return jnp.where(rows <= columns, whole[:half, :half], last), whole[:half, half:], row


def unpacked(first, second, row):
    half = first.shape[0]
    rows = lax.broadcasted_iota(jnp.int32, (half, half), 0)
    columns = lax.broadcasted_iota(jnp.int32, (half, half), 1)
    turned = first.T
    last = jnp.where(rows > columns, first, jnp.where(rows < columns, turned, row))
    return jnp.where(rows <= columns, first, turned), second, last


def kernel(
    nodes, parts, scale,
    subspace, inverse, weights, diag_in, upper_in, out, projected,
    current, blocks, diag, upper, firsts, ups, from_next, from_prior, edge,
    term, ra, rb, pa, pb, qa, qb, field, next_rows, imaged,
    block, mine, pair, pk, grs, zb, res, rest, a, inv,
    load, tip_send, tip_recv, rsa_send, rsa_recv, rsb_send, rsb_recv,
    rsc_send, rsc_recv, rsd_send, rsd_recv,
    aga_send, aga_recv, agb_send, agb_recv, agc_send, agc_recv, agd_send, agd_recv,
    row_send, row_recv, pair_send, pair_recv, grs_send, grs_recv,
    z_send, z_recv, all_send, all_recv, fin_send, fin_recv,
):
    j, p = lax.axis_index("node"), lax.axis_index("rows")
    side = int(round(nodes**0.5))
    x, y = j // side, lax.rem(j, side)
    core = lax.rem(p, 2)
    sibling = p + 1 - 2 * core
    up, down = lax.rem(p + 1, parts), lax.rem(p + parts - 1, parts)
    cross = lax.rem(p + parts - 1 + 2 * core, parts)
    chips = parts // 2
    z = p // 2
    size, columns = current.shape
    band = diag.shape[1]
    piece = size // nodes // 2
    half = columns // 2
    share = half // nodes

    def each(start, stop, act):
        for k in range(start, stop):
            act(k)

    def added(start, stop, add, total):
        for k in range(start, stop):
            total = add(k, total)
        return total

    def turn(value, k, count):
        return lax.rem(value + k, count)

    def copy(src, dst, send, recv, device):
        return pltpu.make_async_remote_copy(
            src_ref=src, dst_ref=dst, send_sem=send, recv_sem=recv, device_id=device, device_id_type=MESH
        )

    loads = [
        pltpu.make_async_copy(subspace, current, load.at[0]),
        pltpu.make_async_copy(inverse, blocks, load.at[1]),
        pltpu.make_async_copy(upper_in, upper, load.at[2]),
        pltpu.make_async_copy(diag_in, diag, load.at[3]),
    ]
    for item in loads:
        item.start()
    barrier = pltpu.get_barrier_semaphore()

    def greet(device):
        pl.semaphore_signal(barrier, inc=1, device_id=device, device_id_type=MESH)

    each(1, chips, lambda k: greet((j, turn(p, 2 * k, parts))))
    each(1, nodes, lambda k: greet((turn(j, k, nodes), p)))
    greet((j, cross))
    greet((j, sibling))
    for item in loads:
        item.wait()
    w0, w1 = weights[0, 0], weights[0, 1]

    def tips(it, ready):
        tip_down, tip_up = tip_copies(it)
        coupling = upper[size - band :, :]
        for part in range(2):
            firsts[part] = dot(blocks[part, :band, :], current[...]).astype(BF16)
        if ready:
            tip_down.start()
        for part in range(2):
            last = dot(blocks[part, size - band :, :], current[...]).astype(BF16).astype(F32)
            ups[part] = dot(coupling, last, 0, 0, precise).astype(BF16)
        if not ready:
            pl.semaphore_wait(barrier, nodes - 1 + chips - 1 + 2)
            tip_down.start()
        tip_up.start()

    def pair_copy(it, m):
        return copy(block.at[m], pair.at[it, m], pair_send.at[it, m], pair_recv.at[it, m], (j, sibling))

    def pack_start(it, m, whole):
        first, second, row = packed(whole)
        mine[m] = jnp.where(core == 0, first, second)
        block[m, :half, :] = jnp.where(core == 0, second, first)
        block[m, half:, :] = jnp.broadcast_to(row, (8, half))
        pair_copy(it, m).start()

    def pack_sum(it, m):
        pair_copy(it, m).wait()
        total = mine[m] + pair[it, m, :half, :]
        pk[m, :, :share, :] = total.reshape(nodes, share, half)
        row = block[m, half:, :] + pair[it, m, half:, :]
        pk[m, :, share:, :] = jnp.broadcast_to(row[None], (nodes, 8, half))

    slice_rows = pl.ds(0, share + 1)

    def grs_copy(it, source, to):
        return copy(
            pk.at[0, to, slice_rows, :], grs.at[it, source, slice_rows, :],
            grs_send.at[it, to], grs_recv.at[it, source], (to, p),
        )

    def z_copy(it, m, source, to):
        here = zb.at[it, m, source, slice_rows, :]
        return copy(here, here, z_send.at[it, m, to], z_recv.at[it, m, source], (j, 2 * to + core))

    def z_start(it, m, value):
        zb[it, m, z, slice_rows, :] = value
        each(1, chips, lambda k: z_copy(it, m, z, turn(z, k, chips)).start())

    def all_copy(it, m, source, to):
        here = res.at[it, m, core, pl.ds(pl.multiple_of(source * share, 8), share), :]
        return copy(here, here, all_send.at[it, m, to], all_recv.at[it, m, source], (to, p))

    def z_finish(it, m):
        def add(k, total):
            source = turn(z, chips - k, chips)
            z_copy(it, m, source, source).wait_recv()
            return total + zb[it, m, source, slice_rows, :]

        total = added(1, chips, add, zb[it, m, z, slice_rows, :])
        rest[it, m] = jnp.broadcast_to(total[share : share + 1, :], (8, half))
        res[it, m, core, pl.ds(pl.multiple_of(j * share, 8), share), :] = total[:share, :]
        each(1, nodes, lambda k: all_copy(it, m, j, turn(j, k, nodes)).start())

    def fin_copy(it, m, which):
        here = res.at[it, m, which]
        return copy(here, here, fin_send.at[it, m], fin_recv.at[it, m], (j, sibling))

    def all_finish(it, m):
        def wait(k):
            source = turn(j, nodes - k, nodes)
            all_copy(it, m, source, source).wait_recv()

        each(1, nodes, wait)
        fin_copy(it, m, core).start()

    def summed(it, m):
        fin_copy(it, m, 1 - core).wait_recv()
        return unpacked(res[it, m, 0], res[it, m, 1], rest[it, m, 0:1, :])

    def project(it):
        first, second, last = summed(it, 1)
        whole = jnp.concatenate(
            [jnp.concatenate([first, second], axis=1), jnp.concatenate([second.T, last], axis=1)], axis=0
        )
        left = dot(inv[it], whole * scale, 1, 0, precise)
        projected[it] = dot(left, inv[it], 1, 1, precise)

    def drained(it):
        row_copy(it).wait_send()

        def over_side(k):
            xx, yy = turn(x, k, side), turn(y, k, side)
            rsa_copy(it, xx, x).wait_send()
            rsc_copy(it, yy, y).wait_send()
            rsd_copy(it, xx, x).wait_send()
            aga_copy(it, xx, x).wait_send()
            agb_copy(it, yy, y).wait_send()
            agc_copy(it, yy, y).wait_send()
            agd_copy(it, xx, x).wait_send()
            each(0, side, lambda g: rsb_copy(it, g, yy, y).wait_send())

        each(1, side, over_side)

        def over_nodes(k):
            to = turn(j, k, nodes)
            grs_copy(it, j, to).wait_send()
            all_copy(it, 0, j, to).wait_send()

        each(1, nodes, over_nodes)
        each(1, chips, lambda k: z_copy(it, 0, z, turn(z, k, chips)).wait_send())
        each(1, chips, lambda k: z_copy(it, 1, z, turn(z, k, chips)).wait_send())
        fin_copy(it, 0, core).wait_send()

    def projected_drained(it):
        each(1, nodes, lambda k: all_copy(it, 1, j, turn(j, k, nodes)).wait_send())
        fin_copy(it, 1, core).wait_send()

    def tip_copies(it):
        return (
            copy(firsts, from_next.at[it], tip_send.at[it, 0], tip_recv.at[it, 0], (j, down)),
            copy(ups, from_prior.at[it], tip_send.at[it, 1], tip_recv.at[it, 1], (j, up)),
        )

    def rsa_copy(it, g, source):
        return copy(term.at[g, :, 0], ra.at[it, source], rsa_send.at[it, g], rsa_recv.at[it, source], (g * side + y, p))

    def rsb_copy(it, g, to, source):
        return copy(
            term.at[g, to, 1], rb.at[it, source, g], rsb_send.at[it, to, g], rsb_recv.at[it, source, g], (x * side + to, p)
        )

    def rsc_copy(it, to, source):
        return copy(pa.at[to], qa.at[it, source], rsc_send.at[it, to], rsc_recv.at[it, source], (x * side + to, p))

    def rsd_copy(it, to, source):
        return copy(pb.at[to], qb.at[it, source], rsd_send.at[it, to], rsd_recv.at[it, source], (to * side + y, p))

    def aga_copy(it, to, source):
        here = field.at[it, source, y, 0]
        return copy(here, here, aga_send.at[it, to], aga_recv.at[it, source], (to * side + y, p))

    def agb_copy(it, to, source):
        here = field.at[it, x, source, 1]
        return copy(here, here, agb_send.at[it, to], agb_recv.at[it, source], (x * side + to, p))

    def agc_copy(it, to, source):
        here = field.at[it, :, source, 0]
        return copy(here, here, agc_send.at[it, to], agc_recv.at[it, source], (x * side + to, p))

    def agd_copy(it, to, source):
        here = field.at[it, source, :, 1]
        return copy(here, here, agd_send.at[it, to], agd_recv.at[it, source], (to * side + y, p))

    def row_copy(it):
        return copy(edge, next_rows.at[it], row_send.at[it], row_recv.at[it], (j, down))

    tile = size // side

    def iteration(it, carry):
        @pl.when(it > 0)
        def _():
            drained(it - 1)

        for g in range(side):
            rows = pl.ds(g * tile, tile)
            value = w0 * dot(blocks[0, rows, :], current[...]) - w1 * dot(blocks[1, rows, :], current[...])
            term[g] = value.reshape(side, 2, piece, columns)

        @pl.when(it > 0)
        def _():
            all_finish(it - 1, 1)
            project(it - 1)
            projected_drained(it - 1)

        tip_down, tip_up = tip_copies(it)
        tip_down.wait()
        coupling = upper[size - band :, :]
        bottom = []
        for part in range(2):
            below = dot(coupling, from_next[it, part].astype(F32), 1, 0, precise).astype(BF16)
            bottom.append(jnp.where(p == parts - 1, 0.0, below.astype(F32)))
        tip_up.wait()
        top = [jnp.where(p == 0, 0.0, from_prior[it, part].astype(F32)) for part in range(2)]
        edges = jnp.concatenate(
            [w0 * e[0] - w1 * e[1] for e in (top, bottom)] + [-w0 * e[1] - w1 * e[0] for e in (top, bottom)], axis=0
        )
        edge_high = edges.astype(BF16)
        edge_low = (edges - edge_high.astype(F32)).astype(BF16)

        def group(t):
            g = turn(x, t + 1, side)
            rows = pl.ds(pl.multiple_of(g * tile, 8), tile)
            corner = jnp.concatenate(
                [blocks[part, rows, at] for part in range(2) for at in (slice(0, band), slice(size - band, size))], axis=1
            )
            change = dot(corner, edge_high) + dot(corner, edge_low)
            term[g] = term[g] + change.reshape(side, 2, piece, columns)

            @pl.when(g != x)
            def _():
                rsa_copy(it, g, x).start()

            each(1, side, lambda k: rsb_copy(it, g, turn(y, k, side), y).start())

        each(0, side, group)

        def add_a(k, total):
            source = turn(x, side - k, side)
            rsa_copy(it, source, source).wait_recv()
            return total + ra[it, source]

        pa[...] = added(1, side, add_a, term[x, :, 0])
        each(1, side, lambda k: rsc_copy(it, turn(y, k, side), y).start())

        def add_b(k, total):
            source = turn(y, side - k, side)
            each(0, side, lambda g: rsb_copy(it, g, source, source).wait_recv())
            return total + rb[it, source]

        pb[...] = added(1, side, add_b, term[:, y, 1])
        each(1, side, lambda k: rsd_copy(it, turn(x, k, side), x).start())

        def add_c(k, total):
            source = turn(y, side - k, side)
            rsc_copy(it, source, source).wait_recv()
            return total + qa[it, source]

        field[it, x, y, 0] = added(1, side, add_c, pa[y])

        def add_d(k, total):
            source = turn(x, side - k, side)
            rsd_copy(it, source, source).wait_recv()
            return total + qb[it, source]

        field[it, x, y, 1] = added(1, side, add_d, pb[x])

        own = field[it, x, y].reshape(2 * piece, columns)
        pack_start(it, 0, dot(own, own, 0, 0, precise))
        pack_sum(it, 0)
        each(1, nodes, lambda k: grs_copy(it, j, turn(j, k, nodes)).start())

        def add_g(k, total):
            source = turn(j, nodes - k, nodes)
            grs_copy(it, source, source).wait_recv()
            return total + grs[it, source, slice_rows, :]

        z_start(it, 0, added(1, nodes, add_g, pk[0, j, slice_rows, :]))

        def ag_first(k):
            aga_copy(it, turn(x, k, side), x).start()
            agb_copy(it, turn(y, k, side), y).start()

        each(1, side, ag_first)

        def ag_first_wait(k):
            aga_copy(it, turn(x, k, side), turn(x, k, side)).wait_recv()

        each(1, side, ag_first_wait)
        each(1, side, lambda k: agc_copy(it, turn(y, k, side), y).start())

        def ag_second_wait(k):
            agb_copy(it, turn(y, k, side), turn(y, k, side)).wait_recv()

        each(1, side, ag_second_wait)
        each(1, side, lambda k: agd_copy(it, turn(x, k, side), x).start())
        z_finish(it, 0)

        def ag_last_wait(k):
            agc_copy(it, turn(y, k, side), turn(y, k, side)).wait_recv()
            agd_copy(it, turn(x, k, side), turn(x, k, side)).wait_recv()

        each(1, side, ag_last_wait)
        whole = field[it].reshape(size, columns)
        edge[...] = whole[:band, :]
        row_copy(it).start()
        tiles = size // band
        for t in range(tiles - 1):
            rows = slice(t * band, t * band + band)
            imaged[rows, :] = dot(0.5 * diag[rows, :], whole[rows, :], 1, 0, precise) + dot(
                upper[rows, :], whole[t * band + band : t * band + 2 * band, :], 1, 0, precise
            )
        all_finish(it, 0)
        rows = slice(size - band, size)
        near = dot(0.5 * diag[rows, :], whole[rows, :], 1, 0, precise)
        row_copy(it).wait_recv()
        after = jnp.where(p == parts - 1, 0.0, next_rows[it])
        imaged[rows, :] = near + dot(upper[rows, :], after, 1, 0, precise)
        product = dot(whole, imaged[...], 0, 0, precise)
        pack_start(it, 1, product + product.T)
        first, second, last = summed(it, 0)
        a[0, :half, :] = first * scale
        a[1, :half, :] = second * scale
        a[0, half:, :] = jnp.zeros((half, half), F32)
        a[1, half:, :] = last * scale
        steps = columns // 8
        for k in range(steps):
            if k == steps // 8 - 1:
                pack_sum(it, 1)
                z_start(it, 1, pk[1, j, slice_rows, :])
            if k == (13 * steps) // 16:
                z_finish(it, 1)
            panel_step(a, k, columns)
        rows = lax.broadcasted_iota(jnp.int32, (columns, columns), 0)
        cols = lax.broadcasted_iota(jnp.int32, (columns, columns), 1)
        factor = jnp.where(rows >= cols, jnp.concatenate([a[0], a[1]], axis=1), 0.0)
        inv[it] = factor
        for g in range(side):
            rows = pl.ds(g * tile, tile)
            value = dot(field[it, g].reshape(tile, columns), factor, 1, 1, precise)
            out[rows, :] = value
            current[rows, :] = value.astype(BF16)

        @pl.when(it < ITERS - 1)
        def _():
            tips(it + 1, True)

        return carry

    tips(0, False)
    lax.fori_loop(0, ITERS, iteration, 0)
    all_finish(ITERS - 1, 1)
    project(ITERS - 1)
    projected_drained(ITERS - 1)
    drained(ITERS - 1)


def finish_kernel(ortho, projected, ortho_out, projected_out, ortho_held, projected_held, come, go):
    count = come.shape[0] // 2
    rows = ortho.shape[0] // count
    wide = projected.shape[1] // count
    places = []
    for k in range(count):
        at = pl.ds(k * rows, rows)
        places.append((ortho.at[at], ortho_held.at[at], ortho_out.at[at]))
    for k in range(count):
        at = pl.ds(k * wide, wide)
        places.append((projected.at[:, at], projected_held.at[:, at], projected_out.at[:, at]))
    into = [pltpu.make_async_copy(a, b, come.at[k]) for k, (a, b, _) in enumerate(places)]
    onward = [pltpu.make_async_copy(b, c, go.at[k]) for k, (_, b, c) in enumerate(places)]
    for item in into:
        item.start()
    for first, second in zip(into, onward):
        first.wait()
        second.start()
    for item in onward:
        item.wait()


def finished(ortho, projected):
    anywhere = pl.BlockSpec(memory_space=pl.ANY)
    return pl.pallas_call(
        finish_kernel,
        out_shape=tuple(jax.ShapeDtypeStruct(v.shape, v.dtype) for v in (ortho, projected)),
        in_specs=[anywhere] * 2,
        out_specs=(anywhere,) * 2,
        scratch_shapes=[pltpu.VMEM(v.shape, v.dtype) for v in (ortho, projected)]
        + [pltpu.SemaphoreType.DMA((8,))] * 2,
        compiler_params=pltpu.CompilerParams(vmem_limit_bytes=62 * 1024 * 1024),
    )(ortho, projected)


def per_device(subspace, inverse, weights, diag_tiles, upper_tiles):
    nodes, parts = lax.axis_size("node"), lax.axis_size("rows")
    rows, columns = subspace.shape
    band = diag_tiles.shape[1]
    side = int(round(nodes**0.5))
    piece = rows // nodes // 2
    half = columns // 2
    share = half // nodes
    chips = parts // 2
    n = ITERS
    vmem, dma = pltpu.VMEM, pltpu.SemaphoreType.DMA
    anywhere = pl.BlockSpec(memory_space=pl.ANY)
    tip = (2, band, columns)
    scratch = [
        vmem((rows, columns), BF16), vmem((2, rows, rows), BF16), vmem((rows, band), F32), vmem((rows, band), F32),
        vmem(tip, BF16), vmem(tip, BF16), vmem((n, *tip), BF16), vmem((n, *tip), BF16), vmem((band, columns), F32),
        vmem((side, side, 2, piece, columns), F32),
        vmem((n, side, side, piece, columns), F32), vmem((n, side, side, piece, columns), F32),
        vmem((side, piece, columns), F32), vmem((side, piece, columns), F32),
        vmem((n, side, piece, columns), F32), vmem((n, side, piece, columns), F32),
        vmem((n, side, side, 2, piece, columns), F32), vmem((n, band, columns), F32), vmem((rows, columns), F32),
        vmem((2, half + 8, half), F32), vmem((2, half, half), F32), vmem((n, 2, half + 8, half), F32),
        vmem((2, nodes, share + 8, half), F32), vmem((n, nodes, share + 8, half), F32),
        vmem((n, 2, chips, share + 8, half), F32), vmem((n, 2, 2, half, half), F32), vmem((n, 2, 8, half), F32),
        vmem((2, columns, half), F32), vmem((n, columns, columns), F32),
        dma((4,)), dma((n, 2)), dma((n, 2)), dma((n, side)), dma((n, side)), dma((n, side, side)), dma((n, side, side)),
    ]
    scratch += [dma((n, side))] * 12
    scratch += [dma((n,)), dma((n,)), dma((n, 2)), dma((n, 2)), dma((n, nodes)), dma((n, nodes))]
    scratch += [dma((n, 2, chips))] * 2 + [dma((n, 2, nodes))] * 2 + [dma((n, 2))] * 2
    results = pl.pallas_call(
        functools.partial(kernel, nodes, parts, 1.0 / (rows * parts)),
        out_shape=(
            jax.ShapeDtypeStruct((rows, columns), F32),
            jax.ShapeDtypeStruct((n, columns, columns), F32),
        ),
        in_specs=[anywhere, anywhere, pl.BlockSpec(memory_space=pltpu.SMEM), anywhere, anywhere],
        out_specs=(pl.BlockSpec(memory_space=pltpu.VMEM),) * 2,
        scratch_shapes=scratch,
        compiler_params=pltpu.CompilerParams(
            collective_id=0, has_side_effects=True, vmem_limit_bytes=62 * 1024 * 1024
        ),
    )(subspace, inverse[0], weights, diag_tiles, upper_tiles)
    return finished(*results)


def solution(mesh):
    placed = (
        P("rows", None),
        P("node", None, "rows", None),
        P("node", None),
        P("rows", None),
        P("rows", None),
    )
    return jax.shard_map(
        per_device, mesh=mesh, in_specs=placed, out_specs=(P("rows", None), P()), check_vma=False
    )
```
